32 devices in a mesh: user: 4 (over y, core), camp: 8 (over z, x).
Axes of the slice: x: 2, y: 2, z: 4, core: 2. Of those that a mesh axis runs over, the one named last changes fastest.
Arguments:
- user_emb: bfloat16 [16384, 256], P('user', 'camp'), may hold values from -6 to 6
- camp_emb: bfloat16 [32768, 256], P('camp', 'user'), may hold values from -6 to 6
- block_ids: int32 [4, 8, 256, 2], P('user', 'camp'), may hold values from 0 to 31, as said below
- spend_caps: int32 [32768], P('camp'), may hold values from 256 to 2047
Outputs:
- allocation: bfloat16 [4, 8, 256, 128, 128], P('user', 'camp')
- camp_duals: float32 [32768], P('camp')
- user_duals: float32 [16384], P('user')
The draws below stay inside these ranges and needn't reach their ends.
Inputs may be any that keep to these rules, and one draw needn't show every extreme that they name: `block_ids`: the blocks of one device are distinct pairs; entry 0 is below 32, entry 1 below 32.
All inputs are finite; a program needn't handle non-finite values.
Results may differ from the reference program's by a relative error of at most 0.008.
Values may be sent and summed in bfloat16 or wider, within the bound.
A program may use at most 128 MiB of HBM per device.

```python
import math
import jax
import jax.numpy as jnp
from jax import lax

E = 256
BLK = 128
NBLK = 256
STEPS = 3
GRID_U = 4
GRID_C = 8
RBLK = 32
CBLK = 32
U = 16384
C = 32768
PAIRS_CAMP = 4096
PAIRS_USER = 8192


def draw_block_ids(key, part):
    device_keys = jax.random.split(jax.random.fold_in(key, 17), GRID_U * GRID_C)

    def one_device(device_key):
        chosen = jax.random.permutation(device_key, RBLK * CBLK)[:NBLK]
        return jnp.stack([chosen // CBLK, chosen % CBLK], axis=-1)
    return jax.vmap(one_device)(device_keys).reshape(GRID_U, GRID_C, NBLK, 2).astype(jnp.int32)


def place_ends(result, own_key, smallest, top_value):
    longest = result.shape.index(max(result.shape))
    spots = []
    for shift in (0, 1):
        where = [jax.random.randint(jax.random.fold_in(own_key, axis), (), 0, length) for axis, length in enumerate(result.shape)]
        where[longest] = (where[longest] + shift) % result.shape[longest]
        spots.append(tuple(where))
    return result.at[spots[0]].set(smallest).at[spots[1]].set(top_value)


def block_scale(stream_key, dims, cuts, smallest, top_value):
    factor_of, own = 1.0, jax.random.fold_in(stream_key, 6)
    for axis_at, shards_of in cuts:
        heights = jnp.exp(jax.random.uniform(jax.random.fold_in(own, axis_at), (shards_of,), jnp.float32, smallest / len(cuts), top_value / len(cuts)))
        factor_of = factor_of * jnp.repeat(heights, dims[axis_at] // shards_of).reshape([-1 if axis == axis_at else 1 for axis in range(len(dims))])
    return factor_of


def bell_draw(stream_key, dims, width, reach, pieces=(), kind=jnp.bfloat16):
    values = width * jax.random.normal(stream_key, dims, jnp.float32)
    if pieces:
        values = values * block_scale(stream_key, dims, pieces, -0.22, 0.18)
    return jnp.clip(values, -reach, reach).astype(kind)


def setup_inputs(seed: int = 0) -> dict:
    key_list = jax.random.split(jax.random.key(seed), 5)
    user_emb = bell_draw(key_list[0], (U, E), 1.0, 6.0, ((0, 4), (1, 8)))
    camp_emb = bell_draw(key_list[1], (C, E), 1.0, 6.0, ((0, 8), (1, 4)))
    block_ids = draw_block_ids(jax.random.fold_in(key_list[4], 71), 0)
    spend_caps = place_ends(jax.random.randint(key_list[3], (C,), PAIRS_CAMP // 16, PAIRS_CAMP // 2), jax.random.fold_in(key_list[3], 1), PAIRS_CAMP // 16, (PAIRS_CAMP // 2) - 1).astype(jnp.int32)
    return dict(user_emb=user_emb, camp_emb=camp_emb, block_ids=block_ids, spend_caps=spend_caps)


step_size = 2.0
user_quota = 0.25

def reference(user_emb, camp_emb, block_ids, spend_caps):
    score_scale = 1.0 / math.sqrt(E)
    user_tiles = user_emb.reshape(GRID_U * RBLK, BLK, E)
    camp_tiles = camp_emb.reshape(GRID_C * CBLK, BLK, E)
    group_row = jnp.arange(GRID_U, dtype=jnp.int32)[:, None, None] * RBLK
    group_col = jnp.arange(GRID_C, dtype=jnp.int32)[None, :, None] * CBLK
    row_index = (group_row + block_ids[..., 0]).reshape(-1, NBLK).astype(jnp.int32)
    col_index = (group_col + block_ids[..., 1]).reshape(-1, NBLK).astype(jnp.int32)

    def score_device(operands):
        rows_here, cols_here = operands
        left = user_tiles[rows_here].astype(jnp.float32)
        right = camp_tiles[cols_here].astype(jnp.float32)
        return (jnp.einsum('bre,bce->brc', left, right) * score_scale).astype(jnp.bfloat16)
    scores = lax.map(score_device, (row_index, col_index))
    cap_float = spend_caps.astype(jnp.float32)

    def allocate(camp_duals, user_duals):
        camp_table = camp_duals.reshape(-1, BLK)
        user_table = user_duals.reshape(-1, BLK)

        def device_alloc(operands):
            tiles, rows_here, cols_here = operands
            return jnp.clip(tiles.astype(jnp.float32) - camp_table[cols_here][:, None, :] - user_table[rows_here][:, :, None], 0.0, 1.0)
        return device_alloc
    camp_duals = jnp.zeros((C,), jnp.float32)
    user_duals = jnp.zeros((U,), jnp.float32)
    for sweep in range(STEPS):
        device_alloc = allocate(camp_duals, user_duals)

        def device_sums(operands):
            shares = device_alloc(operands)
            return (lax.optimization_barrier(jnp.sum(shares, axis=1)), lax.optimization_barrier(jnp.sum(shares, axis=2)))
        col_sums, row_sums = lax.map(device_sums, (scores, row_index, col_index))
        spend = jnp.zeros((C // BLK, BLK), jnp.float32).at[col_index].add(col_sums).reshape(-1)
        load = jnp.zeros((U // BLK, BLK), jnp.float32).at[row_index].add(row_sums).reshape(-1)
        camp_duals = jnp.maximum(0.0, camp_duals + step_size * (spend - cap_float) / PAIRS_CAMP)
        user_duals = jnp.maximum(0.0, user_duals + step_size * (load - user_quota * PAIRS_USER) / PAIRS_USER)
    device_alloc = allocate(camp_duals, user_duals)

    def final_alloc(operands):
        return device_alloc(operands).astype(jnp.bfloat16)
    allocation = lax.map(final_alloc, (scores, row_index, col_index)).reshape(GRID_U, GRID_C, NBLK, BLK, BLK)
    return (allocation, camp_duals, user_duals)
```

```python
import functools
import math

import jax
import jax.numpy as jnp
from jax import lax
from jax.experimental import pallas as pl
from jax.experimental.pallas import tpu as pltpu
from jax.sharding import PartitionSpec as P

STEPS = 3
step_size = 2.0
user_quota = 0.25
BLK = 128
Z_SIZE = 4
CORES = 2
CHUNKS = 8
FINAL_GROUP = 32
MESH = pl.DeviceIdType.MESH


def remote(src, dst, send_sem, recv_sem, axis, target):
    return pltpu.make_async_remote_copy(
        src_ref=src,
        dst_ref=dst,
        send_sem=send_sem,
        recv_sem=recv_sem,
        device_id={axis: target},
        device_id_type=MESH,
    )


class Gather:
    def __init__(self, axis, outer_n, inner_n, src, full, sems):
        self.axis, self.outer_n, self.inner_n = axis, outer_n, inner_n
        self.src, self.full = src, full
        self.own_sem, self.o_send, self.o_recv, self.i_send, self.i_recv = sems
        self.me = lax.axis_index(axis)
        self.o = lax.div(self.me, inner_n)
        self.i = lax.rem(self.me, inner_n)
        self.rows = src.shape[0]
        self.width = src.shape[1] // CHUNKS

    def piece(self, owner, c):
        start = pl.multiple_of(owner * self.rows, self.rows)
        return self.full.at[pl.ds(start, self.rows), pl.ds(c * self.width, self.width)]

    def mine(self, c):
        return self.src.at[:, pl.ds(c * self.width, self.width)]

    def own_copy(self):
        start = pl.multiple_of(self.me * self.rows, self.rows)
        return pltpu.make_async_copy(
            self.src, self.full.at[pl.ds(start, self.rows), :], self.own_sem
        )

    def outer_copy(self, d, c):
        target = lax.rem(self.o + d, self.outer_n) * self.inner_n + self.i
        return remote(
            self.mine(c), self.piece(self.me, c),
            self.o_send.at[d - 1, c], self.o_recv.at[d - 1, c], self.axis, target,
        )

    def inner_copy(self, d, e, c):
        owner = lax.rem(self.o - d + self.outer_n, self.outer_n) * self.inner_n + self.i
        target = self.o * self.inner_n + lax.rem(self.i + e, self.inner_n)
        src = self.mine(c) if d == 0 else self.piece(owner, c)
        return remote(
            src, self.piece(owner, c),
            self.i_send.at[d, e - 1, c], self.i_recv.at[d, e - 1, c], self.axis, target,
        )

    def begin(self, c):
        for d in range(1, self.outer_n):
            self.outer_copy(d, c).start()
        for e in range(1, self.inner_n):
            self.inner_copy(0, e, c).start()

    def forward(self, c):
        for d in range(1, self.outer_n):
            self.outer_copy(d, c).wait_recv()
            for e in range(1, self.inner_n):
                self.inner_copy(d, e, c).start()

    def finish_recv(self, c):
        for d in range(self.outer_n):
            for e in range(1, self.inner_n):
                self.inner_copy(d, e, c).wait_recv()

    def finish_send(self):
        for c in range(CHUNKS):
            for d in range(1, self.outer_n):
                self.outer_copy(d, c).wait_send()
            for d in range(self.outer_n):
                for e in range(1, self.inner_n):
                    self.inner_copy(d, e, c).wait_send()


def spread_users(table, ub):
    columns = table.T
    for i in range(table.shape[0]):
        ub[i] = jnp.broadcast_to(columns[:, i : i + 1], (BLK, BLK))


def spread_camps(table, cb):
    for i in range(table.shape[0]):
        cb[i] = jnp.broadcast_to(table[i : i + 1, :], (8, BLK))


def shares_of(tile, camp_part, user_part):
    x = tile.astype(jnp.float32).reshape(BLK // 8, 8, BLK)
    x = x - camp_part[None] - user_part.reshape(BLK // 8, 8, BLK)
    return jnp.clip(x, 0.0, 1.0)


def parts_of(values):
    high = values.astype(jnp.bfloat16)
    rest = values - high.astype(jnp.float32)
    middle = rest.astype(jnp.bfloat16)
    return high, middle, (rest - middle.astype(jnp.float32)).astype(jnp.bfloat16)


def ascent(
    n_user, n_camp, score_scale, pairs_camp, pairs_user,
    ut, ct, ids_hbm, caps_hbm,
    sc, camp_out, user_out,
    uf, cf, un, cn, ub, cb, colsum, rowsum, spend_slots, load_slots,
    u_own, u_osend, u_orecv, u_isend, u_irecv,
    c_own, c_osend, c_orecv, c_isend, c_irecv,
    s_send, s_recv, l_send, l_recv,
    ids_s, ids_v, caps, small_sem,
):
    me_camp, me_user = lax.axis_index("camp"), lax.axis_index("user")
    blocks = sc.shape[0]
    user_blocks, camp_blocks = un.shape[0], cb.shape[0]

    users = Gather("camp", Z_SIZE, n_camp // Z_SIZE, ut, uf, (u_own, u_osend, u_orecv, u_isend, u_irecv))
    camps = Gather("user", n_user // CORES, CORES, ct, cf, (c_own, c_osend, c_orecv, c_isend, c_irecv))
    small = [
        pltpu.make_async_copy(ids_hbm, ids_s, small_sem.at[0]),
        pltpu.make_async_copy(ids_hbm, ids_v, small_sem.at[1]),
        pltpu.make_async_copy(caps_hbm, caps, small_sem.at[2]),
    ]
    for copy in small:
        copy.start()
    users.own_copy().start()
    camps.own_copy().start()

    barrier = pltpu.get_barrier_semaphore()
    for d in range(1, n_camp):
        pl.semaphore_signal(
            barrier, inc=1, device_id={"camp": lax.rem(me_camp + d, n_camp)}, device_id_type=MESH
        )
    for d in range(1, n_user):
        pl.semaphore_signal(
            barrier, inc=1, device_id={"user": lax.rem(me_user + d, n_user)}, device_id_type=MESH
        )
    pl.semaphore_wait(barrier, n_camp + n_user - 2)

    for c in range(CHUNKS):
        users.begin(c)
        camps.begin(c)
    for c in range(CHUNKS):
        users.forward(c)
        camps.forward(c)
    camps.own_copy().wait()
    users.own_copy().wait()
    for c in range(CHUNKS):
        camps.finish_recv(c)

    @pl.loop(0, camp_blocks)
    def _(i):
        start = pl.multiple_of(i * BLK, BLK)
        cn[i] = cf[:, pl.ds(start, BLK)]

    for c in range(CHUNKS):
        users.finish_recv(c)

        @pl.loop(c * user_blocks // CHUNKS, (c + 1) * user_blocks // CHUNKS)
        def _(i):
            start = pl.multiple_of(i * BLK, BLK)
            un[i] = uf[:, pl.ds(start, BLK)].astype(jnp.float32).T.astype(jnp.bfloat16)

    lanes = lax.broadcasted_iota(jnp.int32, (BLK // 8, 8, BLK), 2)
    for copy in small:
        copy.wait()
    ids_rows = ids_v[0:1, :]
    ids_cols = ids_v[1:2, :]
    user_hits = jnp.where(
        lax.broadcasted_iota(jnp.int32, (user_blocks, blocks), 0) == ids_rows, 1.0, 0.0
    ).astype(jnp.bfloat16)
    camp_hits = jnp.where(
        lax.broadcasted_iota(jnp.int32, (camp_blocks, blocks), 0) == ids_cols, 1.0, 0.0
    ).astype(jnp.bfloat16)
    cap_float = caps[...].astype(jnp.float32)
    camp_duals = jnp.zeros((camp_blocks, BLK), jnp.float32)
    user_duals = jnp.zeros((user_blocks, BLK), jnp.float32)

    ones = jnp.where(
        lax.broadcasted_iota(jnp.int32, (2 * BLK, BLK), 0) // BLK
        == lax.broadcasted_iota(jnp.int32, (2 * BLK, BLK), 1) % 2, 1.0, 0.0,
    )

    def half_sums(half, first):
        sums = jnp.zeros((BLK // 8, 8, BLK), jnp.float32)
        for p in range(BLK // 2):
            pair = []
            for j in (2 * p, 2 * p + 1):
                b = half * BLK + j
                i, k = ids_s[0, b], ids_s[1, b]
                if first:
                    product = jnp.dot(un[i], cn[k], preferred_element_type=jnp.float32)
                    tile = (product * score_scale).astype(jnp.bfloat16)
                    sc[b] = tile
                    x = jnp.clip(tile.astype(jnp.float32), 0.0, 1.0).reshape(BLK // 8, 8, BLK)
                else:
                    x = shares_of(sc[b], cb[k], ub[i])
                colsum[pl.ds(b, 1), :] = jnp.sum(jnp.sum(x, axis=0), axis=0, keepdims=True)
                if p % 2:
                    sums = jnp.where(lanes == j, jnp.sum(x, axis=2, keepdims=True), sums)
                pair.append(x.reshape(BLK, BLK))
            if p % 2 == 0:
                both = jnp.dot(
                    jnp.concatenate(pair, axis=1), ones, preferred_element_type=jnp.float32
                )
                sums = jnp.where(lanes // 2 == p, both.reshape(BLK // 8, 8, BLK), sums)
        rowsum[half] = sums.reshape(BLK, BLK)

    def step(sweep, duals, first):
        camp_duals, user_duals = duals

        @pl.loop(0, blocks // BLK)
        def _(half):
            half_sums(half, first)

        load = 0.0
        for half in range(blocks // BLK):
            for part in parts_of(rowsum[half]):
                load = load + lax.dot_general(
                    user_hits[:, half * BLK : (half + 1) * BLK], part, (((1,), (1,)), ((), ())),
                    preferred_element_type=jnp.float32,
                )
        load_slots[sweep, me_camp] = load
        load_copies = []
        for d in range(n_camp - 1, 0, -1):
            slot = load_slots.at[sweep, me_camp]
            load_copies.append(remote(
                slot, slot, l_send.at[sweep, d - 1], l_recv.at[sweep, d - 1],
                "camp", lax.rem(me_camp + d, n_camp),
            ))
            load_copies[-1].start()
        spend = 0.0
        for part in parts_of(colsum[...]):
            spend = spend + jnp.dot(camp_hits, part, preferred_element_type=jnp.float32)
        spend_slots[sweep, me_user] = spend
        spend_copies = []
        for d in range(1, n_user):
            slot = spend_slots.at[sweep, me_user]
            spend_copies.append(remote(
                slot, slot, s_send.at[sweep, d - 1], s_recv.at[sweep, d - 1],
                "user", lax.rem(me_user + d, n_user),
            ))
            spend_copies[-1].start()
        for copy in spend_copies:
            copy.wait_recv()
        spend = spend_slots[sweep, 0]
        for k in range(1, n_user):
            spend = spend + spend_slots[sweep, k]
        camp_duals = jnp.maximum(
            0.0, camp_duals + step_size * (spend - cap_float) / pairs_camp
        )
        spread_camps(camp_duals, cb)
        for copy in load_copies:
            copy.wait_recv()
        load = load_slots[sweep, 0]
        for k in range(1, n_camp):
            load = load + load_slots[sweep, k]
        user_duals = jnp.maximum(
            0.0, user_duals + step_size * (load - user_quota * pairs_user) / pairs_user
        )
        spread_users(user_duals, ub)
        for copy in load_copies + spend_copies:
            copy.wait_send()
        return camp_duals, user_duals

    duals = step(0, (camp_duals, user_duals), True)
    camp_duals, user_duals = lax.fori_loop(1, STEPS, lambda n, d: step(n, d, False), duals)

    camp_out[...] = camp_duals
    user_out[...] = user_duals
    users.finish_send()
    camps.finish_send()


def final(ids_s, scores, camp_duals, user_duals, alloc, camp_out, user_out, ub, cb, ready, sems):
    spread_users(user_duals[...], ub)
    spread_camps(camp_duals[...], cb)
    camp_out[...] = camp_duals[...]
    user_out[...] = user_duals[...]
    groups = scores.shape[0] // FINAL_GROUP

    def piece(g):
        at = pl.ds(pl.multiple_of(g * FINAL_GROUP, FINAL_GROUP), FINAL_GROUP)
        return pltpu.make_async_copy(ready.at[at], alloc.at[at], sems.at[g])

    @pl.loop(0, groups)
    def _(g):
        for j in range(FINAL_GROUP):
            b = g * FINAL_GROUP + j
            x = shares_of(scores[b], cb[ids_s[1, b]], ub[ids_s[0, b]])
            ready[b] = x.reshape(BLK, BLK).astype(jnp.bfloat16)
        piece(g).start()

    for g in range(groups):
        piece(g).wait()


def in_hbm(array):
    return pltpu.with_memory_space_constraint(array, pltpu.HBM)


def on_device(n_user, n_camp, user_emb, camp_emb, block_ids, spend_caps):
    user_count, camp_count = user_emb.shape[0], camp_emb.shape[0]
    feature_dim = user_emb.shape[1] * n_camp
    user_blocks, camp_blocks = user_count // BLK, camp_count // BLK
    ids = block_ids.reshape(-1, 2).T
    blocks = ids.shape[1]
    pairs_camp = blocks * n_user * BLK * BLK // camp_count
    pairs_user = blocks * n_camp * BLK * BLK // user_count
    caps = spend_caps.reshape(camp_blocks, BLK)
    vmem = pl.BlockSpec(memory_space=pltpu.VMEM)
    hbm = pl.BlockSpec(memory_space=pltpu.HBM)
    dma = pltpu.SemaphoreType.DMA
    x_size, y_size = n_camp // Z_SIZE, n_user // CORES

    def gather_sems(outer, inner):
        return [
            dma,
            dma((max(outer - 1, 1), CHUNKS)), dma((max(outer - 1, 1), CHUNKS)),
            dma((outer, max(inner - 1, 1), CHUNKS)), dma((outer, max(inner - 1, 1), CHUNKS)),
        ]

    scores, camp_duals, user_duals = pl.pallas_call(
        functools.partial(
            ascent, n_user, n_camp, 1.0 / math.sqrt(feature_dim), pairs_camp, pairs_user
        ),
        name="ascent",
        out_shape=(
            jax.ShapeDtypeStruct((blocks, BLK, BLK), jnp.bfloat16),
            jax.ShapeDtypeStruct((camp_blocks, BLK), jnp.float32),
            jax.ShapeDtypeStruct((user_blocks, BLK), jnp.float32),
        ),
        in_specs=[hbm] * 4,
        out_specs=(vmem, vmem, vmem),
        scratch_shapes=[
            pltpu.VMEM((feature_dim, user_count), jnp.bfloat16),
            pltpu.VMEM((feature_dim, camp_count), jnp.bfloat16),
            pltpu.VMEM((user_blocks, BLK, feature_dim), jnp.bfloat16),
            pltpu.VMEM((camp_blocks, feature_dim, BLK), jnp.bfloat16),
            pltpu.VMEM((user_blocks, BLK, BLK), jnp.float32),
            pltpu.VMEM((camp_blocks, 8, BLK), jnp.float32),
            pltpu.VMEM((blocks, BLK), jnp.float32),
            pltpu.VMEM((blocks // BLK, BLK, BLK), jnp.float32),
            pltpu.VMEM((STEPS, n_user, camp_blocks, BLK), jnp.float32),
            pltpu.VMEM((STEPS, n_camp, user_blocks, BLK), jnp.float32),
            *gather_sems(Z_SIZE, x_size),
            *gather_sems(y_size, CORES),
            dma((STEPS, n_user - 1)), dma((STEPS, n_user - 1)),
            dma((STEPS, n_camp - 1)), dma((STEPS, n_camp - 1)),
            pltpu.SMEM((2, blocks), jnp.int32),
            pltpu.VMEM((2, blocks), jnp.int32),
            pltpu.VMEM((camp_blocks, BLK), jnp.int32),
            dma((3,)),
        ],
        compiler_params=pltpu.CompilerParams(
            collective_id=0, has_side_effects=True, vmem_limit_bytes=40 * 2**20
        ),
    )(in_hbm(user_emb.T), in_hbm(camp_emb.T), in_hbm(ids), in_hbm(caps))

    allocation, camp_duals, user_duals = pl.pallas_call(
        final,
        name="final",
        out_shape=(
            jax.ShapeDtypeStruct((blocks, BLK, BLK), jnp.bfloat16),
            jax.ShapeDtypeStruct((camp_blocks, BLK), jnp.float32),
            jax.ShapeDtypeStruct((user_blocks, BLK), jnp.float32),
        ),
        in_specs=[pl.BlockSpec(memory_space=pltpu.SMEM), vmem, vmem, vmem],
        out_specs=(hbm, vmem, vmem),
        scratch_shapes=[
            pltpu.VMEM((user_blocks, BLK, BLK), jnp.float32),
            pltpu.VMEM((camp_blocks, 8, BLK), jnp.float32),
            pltpu.VMEM((blocks, BLK, BLK), jnp.bfloat16),
            dma((blocks // FINAL_GROUP,)),
        ],
        compiler_params=pltpu.CompilerParams(vmem_limit_bytes=24 * 2**20),
    )(in_hbm(ids), scores, camp_duals, user_duals)
    return (
        allocation.reshape(1, 1, blocks, BLK, BLK),
        camp_duals.reshape(-1),
        user_duals.reshape(-1),
    )


def solution(mesh):
    placed = (P("user", "camp"), P("camp", "user"), P("user", "camp", None, None), P("camp"))
    return jax.shard_map(
        functools.partial(on_device, mesh.shape["user"], mesh.shape["camp"]),
        mesh=mesh,
        in_specs=placed,
        out_specs=(P("user", "camp", None, None, None), P("camp"), P("user")),
        check_vma=False,
    )
```

```python
import functools
import math

import jax
import jax.numpy as jnp
from jax import lax
from jax.experimental import pallas as pl
from jax.experimental.pallas import tpu as pltpu
from jax.sharding import PartitionSpec as P

STEPS = 3
step_size = 2.0
user_quota = 0.25
BLK = 128
Z_SIZE = 4
CORES = 2
CHUNKS = 8
LEAD = CHUNKS // 2
EARLY = 2
FINAL_GROUP = 32
MESH = pl.DeviceIdType.MESH


def remote(src, dst, send_sem, recv_sem, axis, target):
    return pltpu.make_async_remote_copy(
        src_ref=src,
        dst_ref=dst,
        send_sem=send_sem,
        recv_sem=recv_sem,
        device_id={axis: target},
        device_id_type=MESH,
    )


class Gather:
    def __init__(self, axis, outer_n, inner_n, src, full, sems):
        self.axis, self.outer_n, self.inner_n = axis, outer_n, inner_n
        self.src, self.full = src, full
        self.own_sem, self.o_send, self.o_recv, self.i_send, self.i_recv = sems
        self.me = lax.axis_index(axis)
        self.o = lax.div(self.me, inner_n)
        self.i = lax.rem(self.me, inner_n)
        self.rows = src.shape[0]
        self.width = src.shape[1] // CHUNKS

    def piece(self, owner, c):
        start = pl.multiple_of(owner * self.rows, self.rows)
        return self.full.at[pl.ds(start, self.rows), pl.ds(c * self.width, self.width)]

    def mine(self, c):
        return self.src.at[:, pl.ds(c * self.width, self.width)]

    def own_copy(self):
        start = pl.multiple_of(self.me * self.rows, self.rows)
        return pltpu.make_async_copy(
            self.src, self.full.at[pl.ds(start, self.rows), :], self.own_sem
        )

    def outer_copy(self, d, c):
        target = lax.rem(self.o + d, self.outer_n) * self.inner_n + self.i
        return remote(
            self.mine(c), self.piece(self.me, c),
            self.o_send.at[d - 1, c], self.o_recv.at[d - 1, c], self.axis, target,
        )

    def inner_copy(self, d, e, c):
        owner = lax.rem(self.o - d + self.outer_n, self.outer_n) * self.inner_n + self.i
        target = self.o * self.inner_n + lax.rem(self.i + e, self.inner_n)
        src = self.mine(c) if d == 0 else self.piece(owner, c)
        return remote(
            src, self.piece(owner, c),
            self.i_send.at[d, e - 1, c], self.i_recv.at[d, e - 1, c], self.axis, target,
        )

    def begin(self, c):
        for d in range(1, self.outer_n):
            self.outer_copy(d, c).start()
        for e in range(1, self.inner_n):
            self.inner_copy(0, e, c).start()

    def forward(self, c):
        for d in range(1, self.outer_n):
            self.outer_copy(d, c).wait_recv()
            for e in range(1, self.inner_n):
                self.inner_copy(d, e, c).start()

    def finish_recv(self, c):
        for d in range(self.outer_n):
            for e in range(1, self.inner_n):
                self.inner_copy(d, e, c).wait_recv()

    def finish_send(self):
        for c in range(CHUNKS):
            for d in range(1, self.outer_n):
                self.outer_copy(d, c).wait_send()
            for d in range(self.outer_n):
                for e in range(1, self.inner_n):
                    self.inner_copy(d, e, c).wait_send()


def spread_users(table, ub):
    columns = table.T
    for i in range(table.shape[0]):
        ub[i] = jnp.broadcast_to(columns[:, i : i + 1], (BLK, BLK))


def spread_camps(table, cb):
    for i in range(table.shape[0]):
        cb[i] = jnp.broadcast_to(table[i : i + 1, :], (8, BLK))


def shares_of(tile, camp_part, user_part):
    x = tile.astype(jnp.float32).reshape(BLK // 8, 8, BLK)
    x = x - camp_part[None] - user_part.reshape(BLK // 8, 8, BLK)
    return jnp.clip(x, 0.0, 1.0)


def parts_of(values):
    high = values.astype(jnp.bfloat16)
    rest = values - high.astype(jnp.float32)
    middle = rest.astype(jnp.bfloat16)
    return high, middle, (rest - middle.astype(jnp.float32)).astype(jnp.bfloat16)


def ascent(
    n_user, n_camp, score_scale, pairs_camp, pairs_user,
    ut, ct, ids_hbm, caps_hbm,
    sc, camp_out, user_out,
    uf, cf, un, dense, ub, cb, colsum, rowsum, spend_slots, load_slots,
    u_own, u_osend, u_orecv, u_isend, u_irecv,
    c_own, c_osend, c_orecv, c_isend, c_irecv,
    s_send, s_recv, l_send, l_recv,
    ids_s, ids_v, caps, small_sem,
):
    me_camp, me_user = lax.axis_index("camp"), lax.axis_index("user")
    blocks = ids_s.shape[1]
    user_blocks, camp_blocks = ub.shape[0], cb.shape[0]

    users = Gather("camp", Z_SIZE, n_camp // Z_SIZE, ut, uf, (u_own, u_osend, u_orecv, u_isend, u_irecv))
    camps = Gather("user", n_user // CORES, CORES, ct, cf, (c_own, c_osend, c_orecv, c_isend, c_irecv))
    small = [
        pltpu.make_async_copy(ids_hbm, ids_s, small_sem.at[0]),
        pltpu.make_async_copy(ids_hbm, ids_v, small_sem.at[1]),
        pltpu.make_async_copy(caps_hbm, caps, small_sem.at[2]),
    ]
    for copy in small:
        copy.start()
    users.own_copy().start()
    camps.own_copy().start()

    barrier = pltpu.get_barrier_semaphore()
    for d in range(1, n_camp):
        pl.semaphore_signal(
            barrier, inc=1, device_id={"camp": lax.rem(me_camp + d, n_camp)}, device_id_type=MESH
        )
    for d in range(1, n_user):
        pl.semaphore_signal(
            barrier, inc=1, device_id={"user": lax.rem(me_user + d, n_user)}, device_id_type=MESH
        )
    pl.semaphore_wait(barrier, n_camp + n_user - 2)

    for c in range(CHUNKS):
        users.begin(c)
        camps.begin(c)

    columns = uf.shape[1] // CHUNKS
    wide = cf.shape[1] // 2

    def turn(c):
        at = pl.ds(pl.multiple_of(c * columns, columns), columns)
        un[at, :] = uf[:, at].astype(jnp.float32).T.astype(jnp.bfloat16)

    def multiply(c, side):
        right = cf[:, side * wide : (side + 1) * wide]
        for r in range(columns // BLK):
            rows = pl.ds(pl.multiple_of(c * columns + r * BLK, BLK), BLK)
            product = jnp.dot(un[rows, :], right, preferred_element_type=jnp.float32)
            tiles = (product * score_scale).astype(jnp.bfloat16)
            first = (c * (columns // BLK) + r) * camp_blocks + side * (wide // BLK)
            for k in range(wide // BLK):
                dense[first + k] = tiles[:, k * BLK : (k + 1) * BLK]

    def arrive(c):
        @pl.when(c + LEAD < CHUNKS)
        def _():
            users.forward(c + LEAD)

        users.finish_recv(c)
        turn(c)

    camps.own_copy().wait()
    users.own_copy().wait()
    for c in range(CHUNKS // 2):
        camps.forward(c)
        users.forward(c)
    for c in range(CHUNKS // 2):
        camps.finish_recv(c)

    @pl.loop(0, EARLY)
    def _(c):
        camps.forward(CHUNKS // 2 + c)
        arrive(c)
        multiply(c, 0)

    for c in range(CHUNKS // 2 + EARLY, CHUNKS):
        camps.forward(c)
    for c in range(CHUNKS // 2, CHUNKS):
        camps.finish_recv(c)

    @pl.loop(0, EARLY)
    def _(c):
        multiply(c, 1)

    @pl.loop(EARLY, CHUNKS)
    def _(c):
        arrive(c)
        multiply(c, 0)
        multiply(c, 1)

    lanes = lax.broadcasted_iota(jnp.int32, (BLK // 8, 8, BLK), 2)
    for copy in small:
        copy.wait()
    ids_rows = ids_v[0:1, :]
    ids_cols = ids_v[1:2, :]
    user_hits = jnp.where(
        lax.broadcasted_iota(jnp.int32, (user_blocks, blocks), 0) == ids_rows, 1.0, 0.0
    ).astype(jnp.bfloat16)
    camp_hits = jnp.where(
        lax.broadcasted_iota(jnp.int32, (camp_blocks, blocks), 0) == ids_cols, 1.0, 0.0
    ).astype(jnp.bfloat16)
    cap_float = caps[...].astype(jnp.float32)
    camp_duals = jnp.zeros((camp_blocks, BLK), jnp.float32)
    user_duals = jnp.zeros((user_blocks, BLK), jnp.float32)

    ones = jnp.where(
        lax.broadcasted_iota(jnp.int32, (2 * BLK, BLK), 0) // BLK
        == lax.broadcasted_iota(jnp.int32, (2 * BLK, BLK), 1) % 2, 1.0, 0.0,
    )

    def half_sums(half, first):
        sums = jnp.zeros((BLK // 8, 8, BLK), jnp.float32)
        for p in range(BLK // 2):
            pair = []
            for j in (2 * p, 2 * p + 1):
                b = half * BLK + j
                i, k = ids_s[0, b], ids_s[1, b]
                if first:
                    tile = dense[i * camp_blocks + k]
                    sc[b] = tile
                    x = jnp.clip(tile.astype(jnp.float32), 0.0, 1.0).reshape(BLK // 8, 8, BLK)
                else:
                    x = shares_of(sc[b], cb[k], ub[i])
                colsum[pl.ds(b, 1), :] = jnp.sum(jnp.sum(x, axis=0), axis=0, keepdims=True)
                if p % 2:
                    sums = jnp.where(lanes == j, jnp.sum(x, axis=2, keepdims=True), sums)
                pair.append(x.reshape(BLK, BLK))
            if p % 2 == 0:
                both = jnp.dot(
                    jnp.concatenate(pair, axis=1), ones, preferred_element_type=jnp.float32
                )
                sums = jnp.where(lanes // 2 == p, both.reshape(BLK // 8, 8, BLK), sums)
        rowsum[half] = sums.reshape(BLK, BLK)

    def step(sweep, duals, first):
        camp_duals, user_duals = duals

        @pl.loop(0, blocks // BLK)
        def _(half):
            half_sums(half, first)

        load = 0.0
        for half in range(blocks // BLK):
            for part in parts_of(rowsum[half]):
                load = load + lax.dot_general(
                    user_hits[:, half * BLK : (half + 1) * BLK], part, (((1,), (1,)), ((), ())),
                    preferred_element_type=jnp.float32,
                )
        load_slots[sweep, me_camp] = load
        load_copies = []
        for d in range(n_camp - 1, 0, -1):
            slot = load_slots.at[sweep, me_camp]
            load_copies.append(remote(
                slot, slot, l_send.at[sweep, d - 1], l_recv.at[sweep, d - 1],
                "camp", lax.rem(me_camp + d, n_camp),
            ))
            load_copies[-1].start()
        spend = 0.0
        for part in parts_of(colsum[...]):
            spend = spend + jnp.dot(camp_hits, part, preferred_element_type=jnp.float32)
        spend_slots[sweep, me_user] = spend
        spend_copies = []
        for d in range(1, n_user):
            slot = spend_slots.at[sweep, me_user]
            spend_copies.append(remote(
                slot, slot, s_send.at[sweep, d - 1], s_recv.at[sweep, d - 1],
                "user", lax.rem(me_user + d, n_user),
            ))
            spend_copies[-1].start()
        for copy in spend_copies:
            copy.wait_recv()
        spend = spend_slots[sweep, 0]
        for k in range(1, n_user):
            spend = spend + spend_slots[sweep, k]
        camp_duals = jnp.maximum(
            0.0, camp_duals + step_size * (spend - cap_float) / pairs_camp
        )
        spread_camps(camp_duals, cb)
        for copy in load_copies:
            copy.wait_recv()
        load = load_slots[sweep, 0]
        for k in range(1, n_camp):
            load = load + load_slots[sweep, k]
        user_duals = jnp.maximum(
            0.0, user_duals + step_size * (load - user_quota * pairs_user) / pairs_user
        )
        spread_users(user_duals, ub)
        for copy in load_copies + spend_copies:
            copy.wait_send()
        return camp_duals, user_duals

    duals = step(0, (camp_duals, user_duals), True)
    camp_duals, user_duals = lax.fori_loop(1, STEPS, lambda n, d: step(n, d, False), duals)

    camp_out[...] = camp_duals
    user_out[...] = user_duals
    users.finish_send()
    camps.finish_send()


def final(ids_s, scores, camp_duals, user_duals, alloc, camp_out, user_out, ub, cb, ready, sems):
    spread_users(user_duals[...], ub)
    spread_camps(camp_duals[...], cb)
    camp_out[...] = camp_duals[...]
    user_out[...] = user_duals[...]
    groups = scores.shape[0] // FINAL_GROUP

    def piece(g):
        at = pl.ds(pl.multiple_of(g * FINAL_GROUP, FINAL_GROUP), FINAL_GROUP)
        return pltpu.make_async_copy(ready.at[at], alloc.at[at], sems.at[g])

    @pl.loop(0, groups)
    def _(g):
        for j in range(FINAL_GROUP):
            b = g * FINAL_GROUP + j
            i, k = ids_s[0, b], ids_s[1, b]
            x = shares_of(scores[b], cb[k], ub[i])
            ready[b] = x.reshape(BLK, BLK).astype(jnp.bfloat16)
        piece(g).start()

    for g in range(groups):
        piece(g).wait()


def in_hbm(array):
    return pltpu.with_memory_space_constraint(array, pltpu.HBM)


def on_device(n_user, n_camp, user_emb, camp_emb, block_ids, spend_caps):
    user_count, camp_count = user_emb.shape[0], camp_emb.shape[0]
    feature_dim = user_emb.shape[1] * n_camp
    user_blocks, camp_blocks = user_count // BLK, camp_count // BLK
    ids = block_ids.reshape(-1, 2).T
    blocks = ids.shape[1]
    pairs_camp = blocks * n_user * BLK * BLK // camp_count
    pairs_user = blocks * n_camp * BLK * BLK // user_count
    caps = spend_caps.reshape(camp_blocks, BLK)
    vmem = pl.BlockSpec(memory_space=pltpu.VMEM)
    hbm = pl.BlockSpec(memory_space=pltpu.HBM)
    dma = pltpu.SemaphoreType.DMA
    x_size, y_size = n_camp // Z_SIZE, n_user // CORES

    def gather_sems(outer, inner):
        return [
            dma,
            dma((max(outer - 1, 1), CHUNKS)), dma((max(outer - 1, 1), CHUNKS)),
            dma((outer, max(inner - 1, 1), CHUNKS)), dma((outer, max(inner - 1, 1), CHUNKS)),
        ]

    scores, camp_duals, user_duals = pl.pallas_call(
        functools.partial(
            ascent, n_user, n_camp, 1.0 / math.sqrt(feature_dim), pairs_camp, pairs_user
        ),
        name="ascent",
        out_shape=(
            jax.ShapeDtypeStruct((blocks, BLK, BLK), jnp.bfloat16),
            jax.ShapeDtypeStruct((camp_blocks, BLK), jnp.float32),
            jax.ShapeDtypeStruct((user_blocks, BLK), jnp.float32),
        ),
        in_specs=[hbm] * 4,
        out_specs=(vmem, vmem, vmem),
        scratch_shapes=[
            pltpu.VMEM((feature_dim, user_count), jnp.bfloat16),
            pltpu.VMEM((feature_dim, camp_count), jnp.bfloat16),
            pltpu.VMEM((user_count, feature_dim), jnp.bfloat16),
            pltpu.VMEM((user_blocks * camp_blocks, BLK, BLK), jnp.bfloat16),
            pltpu.VMEM((user_blocks, BLK, BLK), jnp.float32),
            pltpu.VMEM((camp_blocks, 8, BLK), jnp.float32),
            pltpu.VMEM((blocks, BLK), jnp.float32),
            pltpu.VMEM((blocks // BLK, BLK, BLK), jnp.float32),
            pltpu.VMEM((STEPS, n_user, camp_blocks, BLK), jnp.float32),
            pltpu.VMEM((STEPS, n_camp, user_blocks, BLK), jnp.float32),
            *gather_sems(Z_SIZE, x_size),
            *gather_sems(y_size, CORES),
            dma((STEPS, n_user - 1)), dma((STEPS, n_user - 1)),
            dma((STEPS, n_camp - 1)), dma((STEPS, n_camp - 1)),
            pltpu.SMEM((2, blocks), jnp.int32),
            pltpu.VMEM((2, blocks), jnp.int32),
            pltpu.VMEM((camp_blocks, BLK), jnp.int32),
            dma((3,)),
        ],
        compiler_params=pltpu.CompilerParams(
            collective_id=0, has_side_effects=True, vmem_limit_bytes=43 * 2**20
        ),
    )(in_hbm(user_emb.T), in_hbm(camp_emb.T), in_hbm(ids), in_hbm(caps))

    allocation, camp_duals, user_duals = pl.pallas_call(
        final,
        name="final",
        out_shape=(
            jax.ShapeDtypeStruct((blocks, BLK, BLK), jnp.bfloat16),
            jax.ShapeDtypeStruct((camp_blocks, BLK), jnp.float32),
            jax.ShapeDtypeStruct((user_blocks, BLK), jnp.float32),
        ),
        in_specs=[pl.BlockSpec(memory_space=pltpu.SMEM), vmem, vmem, vmem],
        out_specs=(hbm, vmem, vmem),
        scratch_shapes=[
            pltpu.VMEM((user_blocks, BLK, BLK), jnp.float32),
            pltpu.VMEM((camp_blocks, 8, BLK), jnp.float32),
            pltpu.VMEM((blocks, BLK, BLK), jnp.bfloat16),
            dma((blocks // FINAL_GROUP,)),
        ],
        compiler_params=pltpu.CompilerParams(vmem_limit_bytes=14 * 2**20),
    )(in_hbm(ids), scores, camp_duals, user_duals)
    return (
        allocation.reshape(1, 1, blocks, BLK, BLK),
        camp_duals.reshape(-1),
        user_duals.reshape(-1),
    )


def solution(mesh):
    placed = (P("user", "camp"), P("camp", "user"), P("user", "camp", None, None), P("camp"))
    return jax.shard_map(
        functools.partial(on_device, mesh.shape["user"], mesh.shape["camp"]),
        mesh=mesh,
        in_specs=placed,
        out_specs=(P("user", "camp", None, None, None), P("camp"), P("user")),
        check_vma=False,
    )
```

```python
import functools
import math

import jax
import jax.numpy as jnp
from jax import lax
from jax.experimental import pallas as pl
from jax.experimental.pallas import tpu as pltpu
from jax.sharding import PartitionSpec as P

STEPS = 3
step_size = 2.0
user_quota = 0.25
BLK = 128
Z_SIZE = 4
CORES = 2
CHUNKS = 8
AHEAD = 5
EARLY = 2
FINAL_GROUP = 32
MESH = pl.DeviceIdType.MESH


def remote(src, dst, send_sem, recv_sem, axis, target):
    return pltpu.make_async_remote_copy(
        src_ref=src,
        dst_ref=dst,
        send_sem=send_sem,
        recv_sem=recv_sem,
        device_id={axis: target},
        device_id_type=MESH,
    )


class Gather:
    def __init__(self, axis, outer_n, inner_n, src, full, sems):
        self.axis, self.outer_n, self.inner_n = axis, outer_n, inner_n
        self.src, self.full = src, full
        self.own_sem, self.o_send, self.o_recv, self.i_send, self.i_recv = sems
        self.me = lax.axis_index(axis)
        self.o = lax.div(self.me, inner_n)
        self.i = lax.rem(self.me, inner_n)
        self.rows = src.shape[0]
        self.width = src.shape[1] // CHUNKS

    def piece(self, owner, c):
        start = pl.multiple_of(owner * self.rows, self.rows)
        return self.full.at[pl.ds(start, self.rows), pl.ds(c * self.width, self.width)]

    def mine(self, c):
        return self.src.at[:, pl.ds(c * self.width, self.width)]

    def own_copy(self):
        start = pl.multiple_of(self.me * self.rows, self.rows)
        return pltpu.make_async_copy(
            self.src, self.full.at[pl.ds(start, self.rows), :], self.own_sem
        )

    def outer_copy(self, d, c):
        target = lax.rem(self.o + d, self.outer_n) * self.inner_n + self.i
        return remote(
            self.mine(c), self.piece(self.me, c),
            self.o_send.at[d - 1, c], self.o_recv.at[d - 1, c], self.axis, target,
        )

    def inner_copy(self, d, e, c):
        owner = lax.rem(self.o - d + self.outer_n, self.outer_n) * self.inner_n + self.i
        target = self.o * self.inner_n + lax.rem(self.i + e, self.inner_n)
        src = self.mine(c) if d == 0 else self.piece(owner, c)
        return remote(
            src, self.piece(owner, c),
            self.i_send.at[d, e - 1, c], self.i_recv.at[d, e - 1, c], self.axis, target,
        )

    def begin(self, c):
        for d in range(1, self.outer_n):
            self.outer_copy(d, c).start()
        for e in range(1, self.inner_n):
            self.inner_copy(0, e, c).start()

    def forward(self, c):
        for d in range(1, self.outer_n):
            self.outer_copy(d, c).wait_recv()
            for e in range(1, self.inner_n):
                self.inner_copy(d, e, c).start()

    def finish_recv(self, c):
        for d in range(self.outer_n):
            for e in range(1, self.inner_n):
                self.inner_copy(d, e, c).wait_recv()

    def finish_send(self):
        for c in range(CHUNKS):
            for d in range(1, self.outer_n):
                self.outer_copy(d, c).wait_send()
            for d in range(self.outer_n):
                for e in range(1, self.inner_n):
                    self.inner_copy(d, e, c).wait_send()


class Plane:
    def __init__(self, axis, across, src, full, sems):
        self.axis, self.across, self.src, self.full = axis, across, src, full
        self.own_sem, self.arrived, self.x_own, self.z_own, self.z_on, self.x_on = sems
        self.me = lax.axis_index(axis)
        self.z, self.x = lax.div(self.me, across), lax.rem(self.me, across)
        self.pair = self.z + 1 - 2 * lax.rem(self.z, 2)
        self.other = jnp.where(self.z < 2, 2, 1)
        self.far = jnp.where(self.z < 2, 2, 0)
        self.inner = (self.z == 1) | (self.z == 2)
        self.rows = src.shape[0]
        self.width = src.shape[1] // CHUNKS

    def at(self, z, e=0):
        return z * self.across + lax.rem(self.x + e, self.across)

    def columns(self, c):
        return pl.ds(pl.multiple_of(c * self.width, self.width), self.width)

    def piece(self, owner, c):
        start = pl.multiple_of(owner * self.rows, self.rows)
        return self.full.at[pl.ds(start, self.rows), self.columns(c)]

    def own_copy(self):
        start = pl.multiple_of(self.me * self.rows, self.rows)
        return pltpu.make_async_copy(
            self.src, self.full.at[pl.ds(start, self.rows), :], self.own_sem
        )

    def copy(self, owner, c, sem, target, own=False):
        src = self.src.at[:, self.columns(c)] if own else self.piece(owner, c)
        return remote(
            src, self.piece(owner, c), sem, self.arrived.at[owner, c], self.axis, target
        )

    def wait(self, owner, c):
        self.copy(owner, c, self.x_own.at[0, 0], self.at(self.pair)).wait_recv()

    def across_own(self, c):
        return [
            self.copy(self.me, c, self.x_own.at[e - 1, c], self.at(self.z, e), True)
            for e in range(1, self.across)
        ]

    def along_own(self, c, e=0):
        owner = self.at(self.z, e)
        return [
            self.copy(owner, c, self.z_own.at[e, n, c], self.at(z), e == 0)
            for n, z in enumerate((self.pair, self.other))
        ]

    def along_on(self, c, e=0):
        return [
            self.copy(self.at(self.far + n, e), c, self.z_on.at[n, e, c], self.at(self.pair))
            for n in range(2)
        ]

    def across_on(self, c, which):
        zs = (self.pair,) if which == 0 else (self.far, self.far + 1)
        return [
            self.copy(self.at(z), c, self.x_on.at[which + n, e - 1, c], self.at(self.z, e))
            for n, z in enumerate(zs)
            for e in range(1, self.across)
        ]

    def pass_along(self, c, e=0):
        @pl.when(self.inner)
        def _():
            for n, copy in enumerate(self.along_on(c, e)):
                self.wait(self.at(self.far + n, e), c)
                copy.start()

    def pass_along_last(self, c):
        for e in range(1, self.across):
            self.wait(self.at(self.z, e), c)
            start_all(self.along_own(c, e))
        for e in range(self.across):
            self.pass_along(c, e)

    def pass_across_pair(self, c):
        self.wait(self.at(self.pair), c)
        start_all(self.across_on(c, 0))

    def wait_far(self, c, e=0):
        @pl.when(jnp.logical_not(self.inner))
        def _():
            for n in range(2):
                self.wait(self.at(self.far + n, e), c)

    def pass_across_far(self, c):
        self.wait_far(c)
        start_all(self.across_on(c, 1))

    def finish(self, c):
        for e in range(1, self.across):
            for z in (self.z, self.pair, self.far, self.far + 1):
                self.wait(self.at(z, e), c)

    def finish_last(self, c):
        for e in range(self.across):
            self.wait(self.at(self.pair, e), c)
            self.wait_far(c, e)

    def finish_send(self):
        @pl.loop(0, CHUNKS)
        def _(c):
            sent_all(self.across_own(c))
            sent_all(self.along_own(c))

            @pl.when(self.inner)
            def _():
                sent_all(self.along_on(c))

            @pl.when(c < CHUNKS - 1)
            def _():
                sent_all(self.across_on(c, 0))
                sent_all(self.across_on(c, 1))

        for e in range(1, self.across):
            sent_all(self.along_own(CHUNKS - 1, e))

            @pl.when(self.inner)
            def _(e=e):
                sent_all(self.along_on(CHUNKS - 1, e))


def start_all(copies):
    for copy in copies:
        copy.start()


def sent_all(copies):
    for copy in copies:
        copy.wait_send()


def spread_users(table, ub):
    columns = table.T
    for i in range(table.shape[0]):
        ub[i] = jnp.broadcast_to(columns[:, i : i + 1], (BLK, BLK))


def spread_camps(table, cb):
    for i in range(table.shape[0]):
        cb[i] = jnp.broadcast_to(table[i : i + 1, :], (8, BLK))


def shares_of(tile, camp_part, user_part):
    x = tile.astype(jnp.float32).reshape(BLK // 8, 8, BLK)
    x = x - camp_part[None] - user_part.reshape(BLK // 8, 8, BLK)
    return jnp.clip(x, 0.0, 1.0)


def parts_of(values):
    high = values.astype(jnp.bfloat16)
    rest = values - high.astype(jnp.float32)
    middle = rest.astype(jnp.bfloat16)
    return high, middle, (rest - middle.astype(jnp.float32)).astype(jnp.bfloat16)


def ascent(
    n_user, n_camp, score_scale, pairs_camp, pairs_user,
    ut, ct, ids_hbm, caps_hbm,
    sc, camp_out, user_out,
    uf, cf, un, dense, ub, cb, colsum, rowsum, spend_slots, load_slots,
    u_own, u_arrived, u_xown, u_zown, u_zon, u_xon,
    c_own, c_osend, c_orecv, c_isend, c_irecv,
    s_send, s_recv, l_send, l_recv,
    ids_s, ids_v, caps, small_sem,
):
    me_camp, me_user = lax.axis_index("camp"), lax.axis_index("user")
    blocks = ids_s.shape[1]
    user_blocks, camp_blocks = ub.shape[0], cb.shape[0]

    users = Plane(
        "camp", n_camp // Z_SIZE, ut, uf, (u_own, u_arrived, u_xown, u_zown, u_zon, u_xon)
    )
    camps = Gather("user", n_user // CORES, CORES, ct, cf, (c_own, c_osend, c_orecv, c_isend, c_irecv))
    small = [
        pltpu.make_async_copy(ids_hbm, ids_s, small_sem.at[0]),
        pltpu.make_async_copy(ids_hbm, ids_v, small_sem.at[1]),
        pltpu.make_async_copy(caps_hbm, caps, small_sem.at[2]),
    ]
    for copy in small:
        copy.start()
    users.own_copy().start()
    camps.own_copy().start()

    barrier = pltpu.get_barrier_semaphore()
    for d in range(1, n_camp):
        pl.semaphore_signal(
            barrier, inc=1, device_id={"camp": lax.rem(me_camp + d, n_camp)}, device_id_type=MESH
        )
    for d in range(1, n_user):
        pl.semaphore_signal(
            barrier, inc=1, device_id={"user": lax.rem(me_user + d, n_user)}, device_id_type=MESH
        )
    pl.semaphore_wait(barrier, n_camp + n_user - 2)

    for c in range(CHUNKS):
        start_all(users.across_own(c))
        if c < AHEAD:
            start_all(users.along_own(c))
        camps.begin(c)

    columns = uf.shape[1] // CHUNKS
    wide = cf.shape[1] // 2

    def turn(c):
        at = pl.ds(pl.multiple_of(c * columns, columns), columns)
        un[at, :] = uf[:, at].astype(jnp.float32).T.astype(jnp.bfloat16)

    def multiply(c, side):
        right = cf[:, side * wide : (side + 1) * wide]
        for r in range(columns // BLK):
            rows = pl.ds(pl.multiple_of(c * columns + r * BLK, BLK), BLK)
            product = jnp.dot(un[rows, :], right, preferred_element_type=jnp.float32)
            tiles = (product * score_scale).astype(jnp.bfloat16)
            first = (c * (columns // BLK) + r) * camp_blocks + side * (wide // BLK)
            for k in range(wide // BLK):
                dense[first + k] = tiles[:, k * BLK : (k + 1) * BLK]

    def pass_on(c):
        users.pass_along(c)
        start_all(users.along_own(c + AHEAD))

    last = CHUNKS - 1

    def arrive(t):
        @pl.when(t + 2 < last)
        def _():
            users.pass_along(t + 2)

            @pl.when(t + 2 + AHEAD < CHUNKS)
            def _():
                start_all(users.along_own(t + 2 + AHEAD))

            users.pass_across_pair(t + 2)

        @pl.when(t + 2 == last)
        def _():
            users.pass_along_last(last)

        @pl.when(t + 1 < last)
        def _():
            users.pass_across_far(t + 1)

        @pl.when(t < last)
        def _():
            users.finish(t)

        @pl.when(t == last)
        def _():
            users.finish_last(last)

        turn(t)

    half = CHUNKS // 2
    pass_on(0)
    camps.forward(0)
    camps.forward(1)
    users.pass_across_pair(0)
    users.pass_across_pair(1)
    pass_on(1)
    camps.forward(2)
    users.pass_across_far(0)
    camps.forward(3)
    users.own_copy().wait()
    camps.own_copy().wait()
    for c in range(half):
        camps.finish_recv(c)

    @pl.loop(0, EARLY)
    def _(c):
        camps.forward(half + c)
        arrive(c)
        multiply(c, 0)

    for c in range(half + EARLY, CHUNKS):
        camps.forward(c)
    for c in range(half, CHUNKS):
        camps.finish_recv(c)

    @pl.loop(0, EARLY)
    def _(c):
        multiply(c, 1)

    @pl.loop(EARLY, CHUNKS)
    def _(c):
        arrive(c)
        multiply(c, 0)
        multiply(c, 1)

    lanes = lax.broadcasted_iota(jnp.int32, (BLK // 8, 8, BLK), 2)
    for copy in small:
        copy.wait()
    ids_rows = ids_v[0:1, :]
    ids_cols = ids_v[1:2, :]
    user_hits = jnp.where(
        lax.broadcasted_iota(jnp.int32, (user_blocks, blocks), 0) == ids_rows, 1.0, 0.0
    ).astype(jnp.bfloat16)
    camp_hits = jnp.where(
        lax.broadcasted_iota(jnp.int32, (camp_blocks, blocks), 0) == ids_cols, 1.0, 0.0
    ).astype(jnp.bfloat16)
    cap_float = caps[...].astype(jnp.float32)
    camp_duals = jnp.zeros((camp_blocks, BLK), jnp.float32)
    user_duals = jnp.zeros((user_blocks, BLK), jnp.float32)

    ones = jnp.where(
        lax.broadcasted_iota(jnp.int32, (2 * BLK, BLK), 0) // BLK
        == lax.broadcasted_iota(jnp.int32, (2 * BLK, BLK), 1) % 2, 1.0, 0.0,
    )

    def half_sums(half, first):
        sums = jnp.zeros((BLK // 8, 8, BLK), jnp.float32)
        for p in range(BLK // 2):
            pair = []
            for j in (2 * p, 2 * p + 1):
                b = half * BLK + j
                i, k = ids_s[0, b], ids_s[1, b]
                if first:
                    tile = dense[i * camp_blocks + k]
                    sc[b] = tile
                    x = jnp.clip(tile.astype(jnp.float32), 0.0, 1.0).reshape(BLK // 8, 8, BLK)
                else:
                    x = shares_of(sc[b], cb[k], ub[i])
                colsum[pl.ds(b, 1), :] = jnp.sum(jnp.sum(x, axis=0), axis=0, keepdims=True)
                if p % 2:
                    sums = jnp.where(lanes == j, jnp.sum(x, axis=2, keepdims=True), sums)
                pair.append(x.reshape(BLK, BLK))
            if p % 2 == 0:
                both = jnp.dot(
                    jnp.concatenate(pair, axis=1), ones, preferred_element_type=jnp.float32
                )
                sums = jnp.where(lanes // 2 == p, both.reshape(BLK // 8, 8, BLK), sums)
        rowsum[half] = sums.reshape(BLK, BLK)

    def step(sweep, duals, first):
        camp_duals, user_duals = duals

        @pl.loop(0, blocks // BLK)
        def _(half):
            half_sums(half, first)

        load = 0.0
        for half in range(blocks // BLK):
            for part in parts_of(rowsum[half]):
                load = load + lax.dot_general(
                    user_hits[:, half * BLK : (half + 1) * BLK], part, (((1,), (1,)), ((), ())),
                    preferred_element_type=jnp.float32,
                )
        load_slots[sweep, me_camp] = load
        load_copies = []
        for d in range(n_camp - 1, 0, -1):
            slot = load_slots.at[sweep, me_camp]
            load_copies.append(remote(
                slot, slot, l_send.at[sweep, d - 1], l_recv.at[sweep, d - 1],
                "camp", lax.rem(me_camp + d, n_camp),
            ))
            load_copies[-1].start()
        spend = 0.0
        for part in parts_of(colsum[...]):
            spend = spend + jnp.dot(camp_hits, part, preferred_element_type=jnp.float32)
        spend_slots[sweep, me_user] = spend
        spend_copies = []
        for d in range(1, n_user):
            slot = spend_slots.at[sweep, me_user]
            spend_copies.append(remote(
                slot, slot, s_send.at[sweep, d - 1], s_recv.at[sweep, d - 1],
                "user", lax.rem(me_user + d, n_user),
            ))
            spend_copies[-1].start()
        for copy in spend_copies:
            copy.wait_recv()
        spend = spend_slots[sweep, 0]
        for k in range(1, n_user):
            spend = spend + spend_slots[sweep, k]
        camp_duals = jnp.maximum(
            0.0, camp_duals + step_size * (spend - cap_float) / pairs_camp
        )
        spread_camps(camp_duals, cb)
        for copy in load_copies:
            copy.wait_recv()
        load = load_slots[sweep, 0]
        for k in range(1, n_camp):
            load = load + load_slots[sweep, k]
        user_duals = jnp.maximum(
            0.0, user_duals + step_size * (load - user_quota * pairs_user) / pairs_user
        )
        spread_users(user_duals, ub)
        for copy in load_copies + spend_copies:
            copy.wait_send()
        return camp_duals, user_duals

    duals = step(0, (camp_duals, user_duals), True)
    camp_duals, user_duals = lax.fori_loop(1, STEPS, lambda n, d: step(n, d, False), duals)

    camp_out[...] = camp_duals
    user_out[...] = user_duals
    users.finish_send()
    camps.finish_send()


def final(ids_s, scores, camp_duals, user_duals, alloc, camp_out, user_out, ub, cb, ready, sems):
    spread_users(user_duals[...], ub)
    spread_camps(camp_duals[...], cb)
    camp_out[...] = camp_duals[...]
    user_out[...] = user_duals[...]
    groups = scores.shape[0] // FINAL_GROUP

    def piece(g):
        at = pl.ds(pl.multiple_of(g * FINAL_GROUP, FINAL_GROUP), FINAL_GROUP)
        return pltpu.make_async_copy(ready.at[at], alloc.at[at], sems.at[g])

    @pl.loop(0, groups)
    def _(g):
        for j in range(FINAL_GROUP):
            b = g * FINAL_GROUP + j
            i, k = ids_s[0, b], ids_s[1, b]
            x = shares_of(scores[b], cb[k], ub[i])
            ready[b] = x.reshape(BLK, BLK).astype(jnp.bfloat16)
        piece(g).start()

    for g in range(groups):
        piece(g).wait()


def in_hbm(array):
    return pltpu.with_memory_space_constraint(array, pltpu.HBM)


def on_device(n_user, n_camp, user_emb, camp_emb, block_ids, spend_caps):
    user_count, camp_count = user_emb.shape[0], camp_emb.shape[0]
    feature_dim = user_emb.shape[1] * n_camp
    user_blocks, camp_blocks = user_count // BLK, camp_count // BLK
    ids = block_ids.reshape(-1, 2).T
    blocks = ids.shape[1]
    pairs_camp = blocks * n_user * BLK * BLK // camp_count
    pairs_user = blocks * n_camp * BLK * BLK // user_count
    caps = spend_caps.reshape(camp_blocks, BLK)
    vmem = pl.BlockSpec(memory_space=pltpu.VMEM)
    hbm = pl.BlockSpec(memory_space=pltpu.HBM)
    dma = pltpu.SemaphoreType.DMA
    x_size, y_size = n_camp // Z_SIZE, n_user // CORES

    def gather_sems(outer, inner):
        return [
            dma,
            dma((max(outer - 1, 1), CHUNKS)), dma((max(outer - 1, 1), CHUNKS)),
            dma((outer, max(inner - 1, 1), CHUNKS)), dma((outer, max(inner - 1, 1), CHUNKS)),
        ]

    scores, camp_duals, user_duals = pl.pallas_call(
        functools.partial(
            ascent, n_user, n_camp, 1.0 / math.sqrt(feature_dim), pairs_camp, pairs_user
        ),
        name="ascent",
        out_shape=(
            jax.ShapeDtypeStruct((blocks, BLK, BLK), jnp.bfloat16),
            jax.ShapeDtypeStruct((camp_blocks, BLK), jnp.float32),
            jax.ShapeDtypeStruct((user_blocks, BLK), jnp.float32),
        ),
        in_specs=[hbm] * 4,
        out_specs=(vmem, vmem, vmem),
        scratch_shapes=[
            pltpu.VMEM((feature_dim, user_count), jnp.bfloat16),
            pltpu.VMEM((feature_dim, camp_count), jnp.bfloat16),
            pltpu.VMEM((user_count, feature_dim), jnp.bfloat16),
            pltpu.VMEM((user_blocks * camp_blocks, BLK, BLK), jnp.bfloat16),
            pltpu.VMEM((user_blocks, BLK, BLK), jnp.float32),
            pltpu.VMEM((camp_blocks, 8, BLK), jnp.float32),
            pltpu.VMEM((blocks, BLK), jnp.float32),
            pltpu.VMEM((blocks // BLK, BLK, BLK), jnp.float32),
            pltpu.VMEM((STEPS, n_user, camp_blocks, BLK), jnp.float32),
            pltpu.VMEM((STEPS, n_camp, user_blocks, BLK), jnp.float32),
            dma, dma((n_camp, CHUNKS)), dma((max(x_size - 1, 1), CHUNKS)), dma((x_size, 2, CHUNKS)),
            dma((2, x_size, CHUNKS)), dma((3, max(x_size - 1, 1), CHUNKS)),
            *gather_sems(y_size, CORES),
            dma((STEPS, n_user - 1)), dma((STEPS, n_user - 1)),
            dma((STEPS, n_camp - 1)), dma((STEPS, n_camp - 1)),
            pltpu.SMEM((2, blocks), jnp.int32),
            pltpu.VMEM((2, blocks), jnp.int32),
            pltpu.VMEM((camp_blocks, BLK), jnp.int32),
            dma((3,)),
        ],
        compiler_params=pltpu.CompilerParams(
            collective_id=0, has_side_effects=True, vmem_limit_bytes=43 * 2**20
        ),
    )(in_hbm(user_emb.T), in_hbm(camp_emb.T), in_hbm(ids), in_hbm(caps))

    allocation, camp_duals, user_duals = pl.pallas_call(
        final,
        name="final",
        out_shape=(
            jax.ShapeDtypeStruct((blocks, BLK, BLK), jnp.bfloat16),
            jax.ShapeDtypeStruct((camp_blocks, BLK), jnp.float32),
            jax.ShapeDtypeStruct((user_blocks, BLK), jnp.float32),
        ),
        in_specs=[pl.BlockSpec(memory_space=pltpu.SMEM), vmem, vmem, vmem],
        out_specs=(hbm, vmem, vmem),
        scratch_shapes=[
            pltpu.VMEM((user_blocks, BLK, BLK), jnp.float32),
            pltpu.VMEM((camp_blocks, 8, BLK), jnp.float32),
            pltpu.VMEM((blocks, BLK, BLK), jnp.bfloat16),
            dma((blocks // FINAL_GROUP,)),
        ],
        compiler_params=pltpu.CompilerParams(vmem_limit_bytes=14 * 2**20),
    )(in_hbm(ids), scores, camp_duals, user_duals)
    return (
        allocation.reshape(1, 1, blocks, BLK, BLK),
        camp_duals.reshape(-1),
        user_duals.reshape(-1),
    )


def solution(mesh):
    placed = (P("user", "camp"), P("camp", "user"), P("user", "camp", None, None), P("camp"))
    return jax.shard_map(
        functools.partial(on_device, mesh.shape["user"], mesh.shape["camp"]),
        mesh=mesh,
        in_specs=placed,
        out_specs=(P("user", "camp", None, None, None), P("camp"), P("user")),
        check_vma=False,
    )
```

```python
import functools
import math

import jax
import jax.numpy as jnp
from jax import lax
from jax.experimental import pallas as pl
from jax.experimental.pallas import tpu as pltpu
from jax.sharding import PartitionSpec as P

STEPS = 3
step_size = 2.0
user_quota = 0.25
BLK = 128
Z_SIZE = 4
CORES = 2
CHUNKS = 8
AHEAD = 5
EARLY = 2
FINAL_GROUP = 32
MESH = pl.DeviceIdType.MESH


def remote(src, dst, send_sem, recv_sem, axis, target):
    return pltpu.make_async_remote_copy(
        src_ref=src,
        dst_ref=dst,
        send_sem=send_sem,
        recv_sem=recv_sem,
        device_id={axis: target},
        device_id_type=MESH,
    )


class Gather:
    def __init__(self, axis, outer_n, inner_n, src, full, sems):
        self.axis, self.outer_n, self.inner_n = axis, outer_n, inner_n
        self.src, self.full = src, full
        self.own_sem, self.o_send, self.o_recv, self.i_send, self.i_recv = sems
        self.me = lax.axis_index(axis)
        self.o = lax.div(self.me, inner_n)
        self.i = lax.rem(self.me, inner_n)
        self.rows = src.shape[0]
        self.width = src.shape[1] // CHUNKS

    def piece(self, owner, c):
        start = pl.multiple_of(owner * self.rows, self.rows)
        return self.full.at[pl.ds(start, self.rows), pl.ds(c * self.width, self.width)]

    def mine(self, c):
        return self.src.at[:, pl.ds(c * self.width, self.width)]

    def own_copy(self):
        start = pl.multiple_of(self.me * self.rows, self.rows)
        return pltpu.make_async_copy(
            self.src, self.full.at[pl.ds(start, self.rows), :], self.own_sem
        )

    def outer_copy(self, d, c):
        target = lax.rem(self.o + d, self.outer_n) * self.inner_n + self.i
        return remote(
            self.mine(c), self.piece(self.me, c),
            self.o_send.at[d - 1, c], self.o_recv.at[d - 1, c], self.axis, target,
        )

    def inner_copy(self, d, e, c):
        owner = lax.rem(self.o - d + self.outer_n, self.outer_n) * self.inner_n + self.i
        target = self.o * self.inner_n + lax.rem(self.i + e, self.inner_n)
        src = self.mine(c) if d == 0 else self.piece(owner, c)
        return remote(
            src, self.piece(owner, c),
            self.i_send.at[d, e - 1, c], self.i_recv.at[d, e - 1, c], self.axis, target,
        )

    def begin(self, c):
        for d in range(1, self.outer_n):
            self.outer_copy(d, c).start()
        for e in range(1, self.inner_n):
            self.inner_copy(0, e, c).start()

    def forward(self, c):
        for d in range(1, self.outer_n):
            self.outer_copy(d, c).wait_recv()
            for e in range(1, self.inner_n):
                self.inner_copy(d, e, c).start()

    def finish_recv(self, c):
        for d in range(self.outer_n):
            for e in range(1, self.inner_n):
                self.inner_copy(d, e, c).wait_recv()

    def finish_send(self):
        for c in range(CHUNKS):
            for d in range(1, self.outer_n):
                self.outer_copy(d, c).wait_send()
            for d in range(self.outer_n):
                for e in range(1, self.inner_n):
                    self.inner_copy(d, e, c).wait_send()


class Plane:
    def __init__(self, axis, across, src, full, sems):
        self.axis, self.across, self.src, self.full = axis, across, src, full
        self.own_sem, self.arrived, self.x_own, self.z_own, self.z_on, self.x_on = sems
        self.me = lax.axis_index(axis)
        self.z, self.x = lax.div(self.me, across), lax.rem(self.me, across)
        self.pair = self.z + 1 - 2 * lax.rem(self.z, 2)
        self.other = jnp.where(self.z < 2, 2, 1)
        self.far = jnp.where(self.z < 2, 2, 0)
        self.inner = (self.z == 1) | (self.z == 2)
        self.rows = src.shape[0]
        self.width = src.shape[1] // CHUNKS

    def at(self, z, e=0):
        return z * self.across + lax.rem(self.x + e, self.across)

    def columns(self, c):
        return pl.ds(pl.multiple_of(c * self.width, self.width), self.width)

    def piece(self, owner, c):
        start = pl.multiple_of(owner * self.rows, self.rows)
        return self.full.at[pl.ds(start, self.rows), self.columns(c)]

    def own_copy(self):
        start = pl.multiple_of(self.me * self.rows, self.rows)
        return pltpu.make_async_copy(
            self.src, self.full.at[pl.ds(start, self.rows), :], self.own_sem
        )

    def copy(self, owner, c, sem, target, own=False):
        src = self.src.at[:, self.columns(c)] if own else self.piece(owner, c)
        return remote(
            src, self.piece(owner, c), sem, self.arrived.at[owner, c], self.axis, target
        )

    def wait(self, owner, c):
        self.copy(owner, c, self.x_own.at[0, 0], self.at(self.pair)).wait_recv()

    def across_own(self, c):
        return [
            self.copy(self.me, c, self.x_own.at[e - 1, c], self.at(self.z, e), True)
            for e in range(1, self.across)
        ]

    def along_own(self, c, e=0):
        owner = self.at(self.z, e)
        return [
            self.copy(owner, c, self.z_own.at[e, n, c], self.at(z), e == 0)
            for n, z in enumerate((self.pair, self.other))
        ]

    def along_on(self, c, e=0):
        return [
            self.copy(self.at(self.far + n, e), c, self.z_on.at[n, e, c], self.at(self.pair))
            for n in range(2)
        ]

    def across_on(self, c, which):
        zs = (self.pair,) if which == 0 else (self.far, self.far + 1)
        return [
            self.copy(self.at(z), c, self.x_on.at[which + n, e - 1, c], self.at(self.z, e))
            for n, z in enumerate(zs)
            for e in range(1, self.across)
        ]

    def pass_along(self, c, e=0):
        @pl.when(self.inner)
        def _():
            for n, copy in enumerate(self.along_on(c, e)):
                self.wait(self.at(self.far + n, e), c)
                copy.start()

    def pass_along_last(self, c):
        for e in range(1, self.across):
            self.wait(self.at(self.z, e), c)
            start_all(self.along_own(c, e))
        for e in range(self.across):
            self.pass_along(c, e)

    def pass_across_pair(self, c):
        self.wait(self.at(self.pair), c)
        start_all(self.across_on(c, 0))

    def wait_far(self, c, e=0):
        @pl.when(jnp.logical_not(self.inner))
        def _():
            for n in range(2):
                self.wait(self.at(self.far + n, e), c)

    def pass_across_far(self, c):
        self.wait_far(c)
        start_all(self.across_on(c, 1))

    def finish(self, c):
        for e in range(1, self.across):
            for z in (self.z, self.pair, self.far, self.far + 1):
                self.wait(self.at(z, e), c)

    def finish_last(self, c):
        for e in range(self.across):
            self.wait(self.at(self.pair, e), c)
            self.wait_far(c, e)

    def finish_send(self):
        @pl.loop(0, CHUNKS)
        def _(c):
            sent_all(self.across_own(c))
            sent_all(self.along_own(c))

            @pl.when(self.inner)
            def _():
                sent_all(self.along_on(c))

            @pl.when(c < CHUNKS - 1)
            def _():
                sent_all(self.across_on(c, 0))
                sent_all(self.across_on(c, 1))

        for e in range(1, self.across):
            sent_all(self.along_own(CHUNKS - 1, e))

            @pl.when(self.inner)
            def _(e=e):
                sent_all(self.along_on(CHUNKS - 1, e))


def start_all(copies):
    for copy in copies:
        copy.start()


def sent_all(copies):
    for copy in copies:
        copy.wait_send()


def spread_users(table, ub):
    columns = table.T
    for i in range(table.shape[0]):
        ub[i] = jnp.broadcast_to(columns[:, i : i + 1], (BLK, BLK))


def spread_camps(table, cb):
    for i in range(table.shape[0]):
        cb[i] = jnp.broadcast_to(table[i : i + 1, :], (8, BLK))


def shares_of(tile, camp_part, user_part):
    x = tile.astype(jnp.float32).reshape(BLK // 8, 8, BLK)
    x = x - camp_part[None] - user_part.reshape(BLK // 8, 8, BLK)
    return jnp.clip(x, 0.0, 1.0)


def parts_of(values):
    high = values.astype(jnp.bfloat16)
    rest = values - high.astype(jnp.float32)
    middle = rest.astype(jnp.bfloat16)
    return high, middle, (rest - middle.astype(jnp.float32)).astype(jnp.bfloat16)


def ascent(
    n_user, n_camp, score_scale, pairs_camp, pairs_user,
    ut, ct, ids_hbm, caps_hbm,
    sc, camp_out, user_out,
    uf, cf, un, dense, ub, cb, colsum, rowsum, spend_slots, load_slots,
    u_own, u_arrived, u_xown, u_zown, u_zon, u_xon,
    c_own, c_osend, c_orecv, c_isend, c_irecv,
    s_send, s_recv, l_send, l_recv,
    ids_s, ids_v, caps, small_sem,
):
    me_camp, me_user = lax.axis_index("camp"), lax.axis_index("user")
    blocks = ids_s.shape[1]
    user_blocks, camp_blocks = ub.shape[0], cb.shape[0]

    users = Plane(
        "camp", n_camp // Z_SIZE, ut, uf, (u_own, u_arrived, u_xown, u_zown, u_zon, u_xon)
    )
    camps = Gather("user", n_user // CORES, CORES, ct, cf, (c_own, c_osend, c_orecv, c_isend, c_irecv))
    small = [
        pltpu.make_async_copy(ids_hbm, ids_s, small_sem.at[0]),
        pltpu.make_async_copy(ids_hbm, ids_v, small_sem.at[1]),
        pltpu.make_async_copy(caps_hbm, caps, small_sem.at[2]),
    ]
    for copy in small:
        copy.start()
    users.own_copy().start()
    camps.own_copy().start()

    barrier = pltpu.get_barrier_semaphore()
    for d in range(1, n_camp):
        pl.semaphore_signal(
            barrier, inc=1, device_id={"camp": lax.rem(me_camp + d, n_camp)}, device_id_type=MESH
        )
    for d in range(1, n_user):
        pl.semaphore_signal(
            barrier, inc=1, device_id={"user": lax.rem(me_user + d, n_user)}, device_id_type=MESH
        )
    pl.semaphore_wait(barrier, n_camp + n_user - 2)

    for c in range(CHUNKS):
        start_all(users.across_own(c))
        if c < AHEAD:
            start_all(users.along_own(c))
        camps.begin(c)

    columns = uf.shape[1] // CHUNKS
    wide = cf.shape[1] // 2

    def turn(c):
        at = pl.ds(pl.multiple_of(c * columns, columns), columns)
        un[at, :] = uf[:, at].astype(jnp.float32).T.astype(jnp.bfloat16)

    def multiply(c, side):
        right = cf[:, side * wide : (side + 1) * wide]
        for r in range(columns // BLK):
            rows = pl.ds(pl.multiple_of(c * columns + r * BLK, BLK), BLK)
            product = jnp.dot(un[rows, :], right, preferred_element_type=jnp.float32)
            tiles = (product * score_scale).astype(jnp.bfloat16)
            first = (c * (columns // BLK) + r) * camp_blocks + side * (wide // BLK)
            for k in range(wide // BLK):
                dense[first + k] = tiles[:, k * BLK : (k + 1) * BLK]

    def pass_on(c):
        users.pass_along(c)
        start_all(users.along_own(c + AHEAD))

    last = CHUNKS - 1

    def arrive(t):
        @pl.when(t + 2 < last)
        def _():
            users.pass_across_far(t + 2)

        @pl.when(t + 4 < last)
        def _():
            users.pass_along(t + 4)
            users.pass_across_pair(t + 4)

        @pl.when(t + 4 == last)
        def _():
            users.pass_along_last(last)

        @pl.when(t < last)
        def _():
            users.finish(t)

        @pl.when(t == last)
        def _():
            users.finish_last(last)

        turn(t)

    half = CHUNKS // 2
    pass_on(0)
    camps.forward(0)
    users.pass_across_pair(0)
    users.pass_across_pair(1)
    camps.forward(1)
    pass_on(1)
    camps.forward(2)
    users.pass_across_pair(2)
    pass_on(2)
    users.pass_across_far(0)
    camps.forward(3)
    users.pass_across_pair(3)
    users.pass_along(3)
    users.pass_across_far(1)
    users.own_copy().wait()
    camps.own_copy().wait()
    for c in range(half):
        camps.finish_recv(c)

    @pl.loop(0, EARLY)
    def _(c):
        camps.forward(half + c)
        arrive(c)
        multiply(c, 0)

    for c in range(half + EARLY, CHUNKS):
        camps.forward(c)
    for c in range(half, CHUNKS):
        camps.finish_recv(c)

    @pl.loop(0, EARLY)
    def _(c):
        multiply(c, 1)

    @pl.loop(EARLY, CHUNKS)
    def _(c):
        arrive(c)
        multiply(c, 0)
        multiply(c, 1)

    lanes = lax.broadcasted_iota(jnp.int32, (BLK // 8, 8, BLK), 2)
    for copy in small:
        copy.wait()
    ids_rows = ids_v[0:1, :]
    ids_cols = ids_v[1:2, :]
    user_hits = jnp.where(
        lax.broadcasted_iota(jnp.int32, (user_blocks, blocks), 0) == ids_rows, 1.0, 0.0
    ).astype(jnp.bfloat16)
    camp_hits = jnp.where(
        lax.broadcasted_iota(jnp.int32, (camp_blocks, blocks), 0) == ids_cols, 1.0, 0.0
    ).astype(jnp.bfloat16)
    cap_float = caps[...].astype(jnp.float32)
    camp_duals = jnp.zeros((camp_blocks, BLK), jnp.float32)
    user_duals = jnp.zeros((user_blocks, BLK), jnp.float32)

    ones = jnp.where(
        lax.broadcasted_iota(jnp.int32, (2 * BLK, BLK), 0) // BLK
        == lax.broadcasted_iota(jnp.int32, (2 * BLK, BLK), 1) % 2, 1.0, 0.0,
    )

    def half_sums(half, first):
        sums = jnp.zeros((BLK // 8, 8, BLK), jnp.float32)
        for p in range(BLK // 2):
            pair = []
            for j in (2 * p, 2 * p + 1):
                b = half * BLK + j
                i, k = ids_s[0, b], ids_s[1, b]
                if first:
                    tile = dense[i * camp_blocks + k]
                    sc[b] = tile
                    x = jnp.clip(tile.astype(jnp.float32), 0.0, 1.0).reshape(BLK // 8, 8, BLK)
                else:
                    x = shares_of(sc[b], cb[k], ub[i])
                colsum[pl.ds(b, 1), :] = jnp.sum(jnp.sum(x, axis=0), axis=0, keepdims=True)
                if p % 2:
                    sums = jnp.where(lanes == j, jnp.sum(x, axis=2, keepdims=True), sums)
                pair.append(x.reshape(BLK, BLK))
            if p % 2 == 0:
                both = jnp.dot(
                    jnp.concatenate(pair, axis=1), ones, preferred_element_type=jnp.float32
                )
                sums = jnp.where(lanes // 2 == p, both.reshape(BLK // 8, 8, BLK), sums)
        rowsum[half] = sums.reshape(BLK, BLK)

    def step(sweep, duals, first):
        camp_duals, user_duals = duals

        @pl.loop(0, blocks // BLK)
        def _(half):
            half_sums(half, first)

        load = 0.0
        for half in range(blocks // BLK):
            for part in parts_of(rowsum[half]):
                load = load + lax.dot_general(
                    user_hits[:, half * BLK : (half + 1) * BLK], part, (((1,), (1,)), ((), ())),
                    preferred_element_type=jnp.float32,
                )
        load_slots[sweep, me_camp] = load
        load_copies = []
        for d in range(n_camp - 1, 0, -1):
            slot = load_slots.at[sweep, me_camp]
            load_copies.append(remote(
                slot, slot, l_send.at[sweep, d - 1], l_recv.at[sweep, d - 1],
                "camp", lax.rem(me_camp + d, n_camp),
            ))
            load_copies[-1].start()
        spend = 0.0
        for part in parts_of(colsum[...]):
            spend = spend + jnp.dot(camp_hits, part, preferred_element_type=jnp.float32)
        spend_slots[sweep, me_user] = spend
        spend_copies = []
        for d in range(1, n_user):
            slot = spend_slots.at[sweep, me_user]
            spend_copies.append(remote(
                slot, slot, s_send.at[sweep, d - 1], s_recv.at[sweep, d - 1],
                "user", lax.rem(me_user + d, n_user),
            ))
            spend_copies[-1].start()
        for copy in spend_copies:
            copy.wait_recv()
        spend = spend_slots[sweep, 0]
        for k in range(1, n_user):
            spend = spend + spend_slots[sweep, k]
        camp_duals = jnp.maximum(
            0.0, camp_duals + step_size * (spend - cap_float) / pairs_camp
        )
        spread_camps(camp_duals, cb)
        for copy in load_copies:
            copy.wait_recv()
        load = load_slots[sweep, 0]
        for k in range(1, n_camp):
            load = load + load_slots[sweep, k]
        user_duals = jnp.maximum(
            0.0, user_duals + step_size * (load - user_quota * pairs_user) / pairs_user
        )
        spread_users(user_duals, ub)
        for copy in load_copies + spend_copies:
            copy.wait_send()
        return camp_duals, user_duals

    duals = step(0, (camp_duals, user_duals), True)
    camp_duals, user_duals = lax.fori_loop(1, STEPS, lambda n, d: step(n, d, False), duals)

    camp_out[...] = camp_duals
    user_out[...] = user_duals
    users.finish_send()
    camps.finish_send()


def final(ids_s, scores, camp_duals, user_duals, alloc, camp_out, user_out, ub, cb, ready, sems):
    spread_users(user_duals[...], ub)
    spread_camps(camp_duals[...], cb)
    camp_out[...] = camp_duals[...]
    user_out[...] = user_duals[...]
    groups = scores.shape[0] // FINAL_GROUP

    def piece(g):
        at = pl.ds(pl.multiple_of(g * FINAL_GROUP, FINAL_GROUP), FINAL_GROUP)
        return pltpu.make_async_copy(ready.at[at], alloc.at[at], sems.at[g])

    @pl.loop(0, groups)
    def _(g):
        for j in range(FINAL_GROUP):
            b = g * FINAL_GROUP + j
            i, k = ids_s[0, b], ids_s[1, b]
            x = shares_of(scores[b], cb[k], ub[i])
            ready[b] = x.reshape(BLK, BLK).astype(jnp.bfloat16)
        piece(g).start()

    for g in range(groups):
        piece(g).wait()


def in_hbm(array):
    return pltpu.with_memory_space_constraint(array, pltpu.HBM)


def on_device(n_user, n_camp, user_emb, camp_emb, block_ids, spend_caps):
    user_count, camp_count = user_emb.shape[0], camp_emb.shape[0]
    feature_dim = user_emb.shape[1] * n_camp
    user_blocks, camp_blocks = user_count // BLK, camp_count // BLK
    ids = block_ids.reshape(-1, 2).T
    blocks = ids.shape[1]
    pairs_camp = blocks * n_user * BLK * BLK // camp_count
    pairs_user = blocks * n_camp * BLK * BLK // user_count
    caps = spend_caps.reshape(camp_blocks, BLK)
    vmem = pl.BlockSpec(memory_space=pltpu.VMEM)
    hbm = pl.BlockSpec(memory_space=pltpu.HBM)
    dma = pltpu.SemaphoreType.DMA
    x_size, y_size = n_camp // Z_SIZE, n_user // CORES

    def gather_sems(outer, inner):
        return [
            dma,
            dma((max(outer - 1, 1), CHUNKS)), dma((max(outer - 1, 1), CHUNKS)),
            dma((outer, max(inner - 1, 1), CHUNKS)), dma((outer, max(inner - 1, 1), CHUNKS)),
        ]

    scores, camp_duals, user_duals = pl.pallas_call(
        functools.partial(
            ascent, n_user, n_camp, 1.0 / math.sqrt(feature_dim), pairs_camp, pairs_user
        ),
        name="ascent",
        out_shape=(
            jax.ShapeDtypeStruct((blocks, BLK, BLK), jnp.bfloat16),
            jax.ShapeDtypeStruct((camp_blocks, BLK), jnp.float32),
            jax.ShapeDtypeStruct((user_blocks, BLK), jnp.float32),
        ),
        in_specs=[hbm] * 4,
        out_specs=(vmem, vmem, vmem),
        scratch_shapes=[
            pltpu.VMEM((feature_dim, user_count), jnp.bfloat16),
            pltpu.VMEM((feature_dim, camp_count), jnp.bfloat16),
            pltpu.VMEM((user_count, feature_dim), jnp.bfloat16),
            pltpu.VMEM((user_blocks * camp_blocks, BLK, BLK), jnp.bfloat16),
            pltpu.VMEM((user_blocks, BLK, BLK), jnp.float32),
            pltpu.VMEM((camp_blocks, 8, BLK), jnp.float32),
            pltpu.VMEM((blocks, BLK), jnp.float32),
            pltpu.VMEM((blocks // BLK, BLK, BLK), jnp.float32),
            pltpu.VMEM((STEPS, n_user, camp_blocks, BLK), jnp.float32),
            pltpu.VMEM((STEPS, n_camp, user_blocks, BLK), jnp.float32),
            dma, dma((n_camp, CHUNKS)), dma((max(x_size - 1, 1), CHUNKS)), dma((x_size, 2, CHUNKS)),
            dma((2, x_size, CHUNKS)), dma((3, max(x_size - 1, 1), CHUNKS)),
            *gather_sems(y_size, CORES),
            dma((STEPS, n_user - 1)), dma((STEPS, n_user - 1)),
            dma((STEPS, n_camp - 1)), dma((STEPS, n_camp - 1)),
            pltpu.SMEM((2, blocks), jnp.int32),
            pltpu.VMEM((2, blocks), jnp.int32),
            pltpu.VMEM((camp_blocks, BLK), jnp.int32),
            dma((3,)),
        ],
        compiler_params=pltpu.CompilerParams(
            collective_id=0, has_side_effects=True, vmem_limit_bytes=43 * 2**20
        ),
    )(in_hbm(user_emb.T), in_hbm(camp_emb.T), in_hbm(ids), in_hbm(caps))

    allocation, camp_duals, user_duals = pl.pallas_call(
        final,
        name="final",
        out_shape=(
            jax.ShapeDtypeStruct((blocks, BLK, BLK), jnp.bfloat16),
            jax.ShapeDtypeStruct((camp_blocks, BLK), jnp.float32),
            jax.ShapeDtypeStruct((user_blocks, BLK), jnp.float32),
        ),
        in_specs=[pl.BlockSpec(memory_space=pltpu.SMEM), vmem, vmem, vmem],
        out_specs=(hbm, vmem, vmem),
        scratch_shapes=[
            pltpu.VMEM((user_blocks, BLK, BLK), jnp.float32),
            pltpu.VMEM((camp_blocks, 8, BLK), jnp.float32),
            pltpu.VMEM((blocks, BLK, BLK), jnp.bfloat16),
            dma((blocks // FINAL_GROUP,)),
        ],
        compiler_params=pltpu.CompilerParams(vmem_limit_bytes=14 * 2**20),
    )(in_hbm(ids), scores, camp_duals, user_duals)
    return (
        allocation.reshape(1, 1, blocks, BLK, BLK),
        camp_duals.reshape(-1),
        user_duals.reshape(-1),
    )


def solution(mesh):
    placed = (P("user", "camp"), P("camp", "user"), P("user", "camp", None, None), P("camp"))
    return jax.shard_map(
        functools.partial(on_device, mesh.shape["user"], mesh.shape["camp"]),
        mesh=mesh,
        in_specs=placed,
        out_specs=(P("user", "camp", None, None, None), P("camp"), P("user")),
        check_vma=False,
    )
```

```python
import functools
import math

import jax
import jax.numpy as jnp
from jax import lax
from jax.experimental import pallas as pl
from jax.experimental.pallas import tpu as pltpu
from jax.sharding import PartitionSpec as P

STEPS = 3
step_size = 2.0
user_quota = 0.25
BLK = 128
Z_SIZE = 4
CORES = 2
CHUNKS = 8
AHEAD = 5
EARLY = 2
FINAL_GROUP = 16
MESH = pl.DeviceIdType.MESH


def remote(src, dst, send_sem, recv_sem, axis, target):
    return pltpu.make_async_remote_copy(
        src_ref=src,
        dst_ref=dst,
        send_sem=send_sem,
        recv_sem=recv_sem,
        device_id={axis: target},
        device_id_type=MESH,
    )


class Gather:
    def __init__(self, axis, outer_n, inner_n, src, full, sems):
        self.axis, self.outer_n, self.inner_n = axis, outer_n, inner_n
        self.src, self.full = src, full
        self.own_sem, self.o_send, self.o_recv, self.i_send, self.i_recv = sems
        self.me = lax.axis_index(axis)
        self.o = lax.div(self.me, inner_n)
        self.i = lax.rem(self.me, inner_n)
        self.rows = src.shape[0]
        self.width = src.shape[1] // CHUNKS

    def piece(self, owner, c):
        start = pl.multiple_of(owner * self.rows, self.rows)
        return self.full.at[pl.ds(start, self.rows), pl.ds(c * self.width, self.width)]

    def mine(self, c):
        return self.src.at[:, pl.ds(c * self.width, self.width)]

    def own_copy(self):
        start = pl.multiple_of(self.me * self.rows, self.rows)
        return pltpu.make_async_copy(
            self.src, self.full.at[pl.ds(start, self.rows), :], self.own_sem
        )

    def outer_copy(self, d, c):
        target = lax.rem(self.o + d, self.outer_n) * self.inner_n + self.i
        return remote(
            self.mine(c), self.piece(self.me, c),
            self.o_send.at[d - 1, c], self.o_recv.at[d - 1, c], self.axis, target,
        )

    def inner_copy(self, d, e, c):
        owner = lax.rem(self.o - d + self.outer_n, self.outer_n) * self.inner_n + self.i
        target = self.o * self.inner_n + lax.rem(self.i + e, self.inner_n)
        src = self.mine(c) if d == 0 else self.piece(owner, c)
        return remote(
            src, self.piece(owner, c),
            self.i_send.at[d, e - 1, c], self.i_recv.at[d, e - 1, c], self.axis, target,
        )

    def begin(self, c):
        for d in range(1, self.outer_n):
            self.outer_copy(d, c).start()
        for e in range(1, self.inner_n):
            self.inner_copy(0, e, c).start()

    def forward(self, c):
        for d in range(1, self.outer_n):
            self.outer_copy(d, c).wait_recv()
            for e in range(1, self.inner_n):
                self.inner_copy(d, e, c).start()

    def finish_recv(self, c):
        for d in range(self.outer_n):
            for e in range(1, self.inner_n):
                self.inner_copy(d, e, c).wait_recv()

    def finish_send(self):
        for c in range(CHUNKS):
            for d in range(1, self.outer_n):
                self.outer_copy(d, c).wait_send()
            for d in range(self.outer_n):
                for e in range(1, self.inner_n):
                    self.inner_copy(d, e, c).wait_send()


class Plane:
    def __init__(self, axis, across, src, full, sems):
        self.axis, self.across, self.src, self.full = axis, across, src, full
        self.own_sem, self.arrived, self.x_own, self.z_own, self.z_on, self.x_on = sems
        self.me = lax.axis_index(axis)
        self.z, self.x = lax.div(self.me, across), lax.rem(self.me, across)
        self.pair = self.z + 1 - 2 * lax.rem(self.z, 2)
        self.other = jnp.where(self.z < 2, 2, 1)
        self.far = jnp.where(self.z < 2, 2, 0)
        self.inner = (self.z == 1) | (self.z == 2)
        self.rows = src.shape[0]
        self.width = src.shape[1] // CHUNKS

    def at(self, z, e=0):
        return z * self.across + lax.rem(self.x + e, self.across)

    def columns(self, c):
        return pl.ds(pl.multiple_of(c * self.width, self.width), self.width)

    def piece(self, owner, c):
        start = pl.multiple_of(owner * self.rows, self.rows)
        return self.full.at[pl.ds(start, self.rows), self.columns(c)]

    def own_copy(self):
        start = pl.multiple_of(self.me * self.rows, self.rows)
        return pltpu.make_async_copy(
            self.src, self.full.at[pl.ds(start, self.rows), :], self.own_sem
        )

    def copy(self, owner, c, sem, target, own=False):
        src = self.src.at[:, self.columns(c)] if own else self.piece(owner, c)
        return remote(
            src, self.piece(owner, c), sem, self.arrived.at[owner, c], self.axis, target
        )

    def wait(self, owner, c):
        self.copy(owner, c, self.x_own.at[0, 0], self.at(self.pair)).wait_recv()

    def across_own(self, c):
        return [
            self.copy(self.me, c, self.x_own.at[e - 1, c], self.at(self.z, e), True)
            for e in range(1, self.across)
        ]

    def along_own(self, c, e=0):
        owner = self.at(self.z, e)
        return [
            self.copy(owner, c, self.z_own.at[e, n, c], self.at(z), e == 0)
            for n, z in enumerate((self.pair, self.other))
        ]

    def along_on(self, c, e=0):
        return [
            self.copy(self.at(self.far + n, e), c, self.z_on.at[n, e, c], self.at(self.pair))
            for n in range(2)
        ]

    def across_on(self, c, which):
        zs = (self.pair,) if which == 0 else (self.far, self.far + 1)
        return [
            self.copy(self.at(z), c, self.x_on.at[which + n, e - 1, c], self.at(self.z, e))
            for n, z in enumerate(zs)
            for e in range(1, self.across)
        ]

    def pass_along(self, c, e=0):
        @pl.when(self.inner)
        def _():
            for n, copy in enumerate(self.along_on(c, e)):
                self.wait(self.at(self.far + n, e), c)
                copy.start()

    def pass_along_last(self, c):
        for e in range(1, self.across):
            self.wait(self.at(self.z, e), c)
            start_all(self.along_own(c, e))
        for e in range(self.across):
            self.pass_along(c, e)

    def pass_across_pair(self, c):
        self.wait(self.at(self.pair), c)
        start_all(self.across_on(c, 0))

    def wait_far(self, c, e=0):
        @pl.when(jnp.logical_not(self.inner))
        def _():
            for n in range(2):
                self.wait(self.at(self.far + n, e), c)

    def pass_across_far(self, c):
        self.wait_far(c)
        start_all(self.across_on(c, 1))

    def finish(self, c):
        for e in range(1, self.across):
            for z in (self.z, self.pair, self.far, self.far + 1):
                self.wait(self.at(z, e), c)

    def finish_last(self, c):
        for e in range(self.across):
            self.wait(self.at(self.pair, e), c)
            self.wait_far(c, e)

    def finish_send(self):
        @pl.loop(0, CHUNKS)
        def _(c):
            sent_all(self.across_own(c))
            sent_all(self.along_own(c))

            @pl.when(self.inner)
            def _():
                sent_all(self.along_on(c))

            @pl.when(c < CHUNKS - 1)
            def _():
                sent_all(self.across_on(c, 0))
                sent_all(self.across_on(c, 1))

        for e in range(1, self.across):
            sent_all(self.along_own(CHUNKS - 1, e))

            @pl.when(self.inner)
            def _(e=e):
                sent_all(self.along_on(CHUNKS - 1, e))


def start_all(copies):
    for copy in copies:
        copy.start()


def sent_all(copies):
    for copy in copies:
        copy.wait_send()


def spread_users(table, ub):
    columns = table.T
    for i in range(table.shape[0]):
        ub[i] = jnp.broadcast_to(columns[:, i : i + 1], (BLK, BLK))


def spread_camps(table, cb):
    for i in range(table.shape[0]):
        cb[i] = jnp.broadcast_to(table[i : i + 1, :], (8, BLK))


def shares_of(tile, camp_part, user_part):
    x = tile.astype(jnp.float32).reshape(BLK // 8, 8, BLK)
    x = x - camp_part[None] - user_part.reshape(BLK // 8, 8, BLK)
    return jnp.clip(x, 0.0, 1.0)


def parts_of(values):
    high = values.astype(jnp.bfloat16)
    return high, (values - high.astype(jnp.float32)).astype(jnp.bfloat16)


def ascent(
    n_user, n_camp, score_scale, pairs_camp, pairs_user,
    ut, ct, ids_hbm, caps_hbm,
    sc, ub, cb, camp_out, user_out,
    uf, cf, un, dense, colsum, rowsum, spend_slots, load_slots,
    u_own, u_arrived, u_xown, u_zown, u_zon, u_xon,
    c_own, c_osend, c_orecv, c_isend, c_irecv,
    s_send, s_recv, l_send, l_recv,
    ids_s, ids_v, caps, small_sem,
):
    me_camp, me_user = lax.axis_index("camp"), lax.axis_index("user")
    blocks = ids_s.shape[1]
    user_blocks, camp_blocks = ub.shape[0], cb.shape[0]

    users = Plane(
        "camp", n_camp // Z_SIZE, ut, uf, (u_own, u_arrived, u_xown, u_zown, u_zon, u_xon)
    )
    camps = Gather("user", n_user // CORES, CORES, ct, cf, (c_own, c_osend, c_orecv, c_isend, c_irecv))
    small = [
        pltpu.make_async_copy(ids_hbm, ids_s, small_sem.at[0]),
        pltpu.make_async_copy(ids_hbm, ids_v, small_sem.at[1]),
        pltpu.make_async_copy(caps_hbm, caps, small_sem.at[2]),
    ]
    for copy in small:
        copy.start()
    users.own_copy().start()
    camps.own_copy().start()

    barrier = pltpu.get_barrier_semaphore()
    for d in range(1, n_camp):
        pl.semaphore_signal(
            barrier, inc=1, device_id={"camp": lax.rem(me_camp + d, n_camp)}, device_id_type=MESH
        )
    for d in range(1, n_user):
        pl.semaphore_signal(
            barrier, inc=1, device_id={"user": lax.rem(me_user + d, n_user)}, device_id_type=MESH
        )
    pl.semaphore_wait(barrier, n_camp + n_user - 2)

    for c in range(CHUNKS):
        start_all(users.across_own(c))
        if c < AHEAD:
            start_all(users.along_own(c))
        camps.begin(c)

    columns = uf.shape[1] // CHUNKS
    wide = cf.shape[1] // 2

    def turn(c):
        at = pl.ds(pl.multiple_of(c * columns, columns), columns)
        un[at, :] = uf[:, at].astype(jnp.float32).T.astype(jnp.bfloat16)

    def multiply(c, side):
        right = cf[:, side * wide : (side + 1) * wide]
        for r in range(columns // BLK):
            rows = pl.ds(pl.multiple_of(c * columns + r * BLK, BLK), BLK)
            product = jnp.dot(un[rows, :], right, preferred_element_type=jnp.float32)
            tiles = (product * score_scale).astype(jnp.bfloat16)
            first = (c * (columns // BLK) + r) * camp_blocks + side * (wide // BLK)
            for k in range(wide // BLK):
                dense[first + k] = tiles[:, k * BLK : (k + 1) * BLK]

    def pass_on(c):
        users.pass_along(c)
        start_all(users.along_own(c + AHEAD))

    last = CHUNKS - 1

    def arrive(t):
        @pl.when(t + 2 < last)
        def _():
            users.pass_across_far(t + 2)

        @pl.when(t + 4 < last)
        def _():
            users.pass_along(t + 4)
            users.pass_across_pair(t + 4)

        @pl.when(t + 4 == last)
        def _():
            users.pass_along_last(last)

        c = jnp.where(t < last - 1, t, 2 * last - 1 - t)

        @pl.when(c < last)
        def _():
            users.finish(c)

        @pl.when(c == last)
        def _():
            users.finish_last(last)

        turn(c)
        return c

    half = CHUNKS // 2
    pass_on(0)
    camps.forward(0)
    users.pass_across_pair(0)
    users.pass_across_pair(1)
    camps.forward(1)
    pass_on(1)
    camps.forward(2)
    users.pass_across_pair(2)
    pass_on(2)
    users.pass_across_far(0)
    camps.forward(3)
    users.pass_across_pair(3)
    users.pass_along(3)
    users.pass_across_far(1)
    users.own_copy().wait()
    camps.own_copy().wait()
    for c in range(half):
        camps.finish_recv(c)

    @pl.loop(0, EARLY)
    def _(c):
        camps.forward(half + c)
        arrive(c)
        multiply(c, 0)

    for c in range(half + EARLY, CHUNKS):
        camps.forward(c)
    for c in range(half, CHUNKS):
        camps.finish_recv(c)

    @pl.loop(0, EARLY)
    def _(c):
        multiply(c, 1)

    @pl.loop(EARLY, CHUNKS)
    def _(c):
        c = arrive(c)
        multiply(c, 0)
        multiply(c, 1)

    lanes = lax.broadcasted_iota(jnp.int32, (BLK // 8, 8, BLK), 2)
    for copy in small:
        copy.wait()
    ids_rows = ids_v[0:1, :]
    ids_cols = ids_v[1:2, :]
    user_hits = jnp.where(
        lax.broadcasted_iota(jnp.int32, (user_blocks, blocks), 0) == ids_rows, 1.0, 0.0
    ).astype(jnp.bfloat16)
    camp_hits = jnp.where(
        lax.broadcasted_iota(jnp.int32, (camp_blocks, blocks), 0) == ids_cols, 1.0, 0.0
    ).astype(jnp.bfloat16)
    cap_float = caps[...].astype(jnp.float32)
    camp_duals = jnp.zeros((camp_blocks, BLK), jnp.float32)
    user_duals = jnp.zeros((user_blocks, BLK), jnp.float32)

    ones = jnp.where(
        lax.broadcasted_iota(jnp.int32, (2 * BLK, BLK), 0) // BLK
        == lax.broadcasted_iota(jnp.int32, (2 * BLK, BLK), 1) % 2, 1.0, 0.0,
    )

    def half_sums(half, first):
        sums = jnp.zeros((BLK // 8, 8, BLK), jnp.float32)
        for p in range(BLK // 2):
            pair = []
            for j in (2 * p, 2 * p + 1):
                b = half * BLK + j
                i, k = ids_s[0, b], ids_s[1, b]
                if first:
                    tile = dense[i * camp_blocks + k]
                    sc[b] = tile
                    x = jnp.clip(tile.astype(jnp.float32), 0.0, 1.0).reshape(BLK // 8, 8, BLK)
                else:
                    x = shares_of(sc[b], cb[k], ub[i])
                colsum[pl.ds(b, 1), :] = jnp.sum(jnp.sum(x, axis=0), axis=0, keepdims=True)
                if p % 2:
                    sums = jnp.where(lanes == j, jnp.sum(x, axis=2, keepdims=True), sums)
                pair.append(x.reshape(BLK, BLK))
            if p % 2 == 0:
                both = jnp.dot(
                    jnp.concatenate(pair, axis=1), ones, preferred_element_type=jnp.float32
                )
                sums = jnp.where(lanes // 2 == p, both.reshape(BLK // 8, 8, BLK), sums)
        rowsum[half] = sums.reshape(BLK, BLK)

    def step(sweep, duals, first):
        camp_duals, user_duals = duals

        @pl.loop(0, blocks // BLK)
        def _(half):
            half_sums(half, first)

        load = 0.0
        for half in range(blocks // BLK):
            hits = user_hits[:, half * BLK : (half + 1) * BLK]
            load = load + lax.dot_general(
                jnp.concatenate([hits, hits], axis=1),
                jnp.concatenate(parts_of(rowsum[half]), axis=1),
                (((1,), (1,)), ((), ())), preferred_element_type=jnp.float32,
            )
        load_slots[sweep, me_camp] = load
        load_copies = []
        for d in range(n_camp - 1, 0, -1):
            slot = load_slots.at[sweep, me_camp]
            load_copies.append(remote(
                slot, slot, l_send.at[sweep, d - 1], l_recv.at[sweep, d - 1],
                "camp", lax.rem(me_camp + d, n_camp),
            ))
            load_copies[-1].start()
        spend = jnp.dot(
            jnp.concatenate([camp_hits, camp_hits], axis=1),
            jnp.concatenate(parts_of(colsum[...]), axis=0), preferred_element_type=jnp.float32,
        )
        spend_slots[sweep, me_user] = spend
        spend_copies = []
        for d in range(1, n_user):
            slot = spend_slots.at[sweep, me_user]
            spend_copies.append(remote(
                slot, slot, s_send.at[sweep, d - 1], s_recv.at[sweep, d - 1],
                "user", lax.rem(me_user + d, n_user),
            ))
            spend_copies[-1].start()
        for copy in spend_copies:
            copy.wait_recv()
        spend = spend_slots[sweep, 0]
        for k in range(1, n_user):
            spend = spend + spend_slots[sweep, k]
        camp_duals = jnp.maximum(
            0.0, camp_duals + step_size * (spend - cap_float) / pairs_camp
        )
        spread_camps(camp_duals, cb)
        for copy in load_copies:
            copy.wait_recv()
        load = load_slots[sweep, 0]
        for k in range(1, n_camp):
            load = load + load_slots[sweep, k]
        user_duals = jnp.maximum(
            0.0, user_duals + step_size * (load - user_quota * pairs_user) / pairs_user
        )
        spread_users(user_duals, ub)
        for copy in load_copies + spend_copies:
            copy.wait_send()
        return camp_duals, user_duals

    duals = step(0, (camp_duals, user_duals), True)
    camp_duals, user_duals = lax.fori_loop(1, STEPS, lambda n, d: step(n, d, False), duals)

    camp_out[...] = camp_duals
    user_out[...] = user_duals
    users.finish_send()
    camps.finish_send()


def final(ids_s, scores, ub, cb, camp_duals, user_duals, alloc, camp_out, user_out, ready, sems):
    camp_out[...] = camp_duals[...]
    user_out[...] = user_duals[...]
    groups = scores.shape[0] // FINAL_GROUP

    def piece(g):
        at = pl.ds(pl.multiple_of(g * FINAL_GROUP, FINAL_GROUP), FINAL_GROUP)
        return pltpu.make_async_copy(ready.at[at], alloc.at[at], sems.at[g])

    @pl.loop(0, groups)
    def _(g):
        for j in range(FINAL_GROUP):
            b = g * FINAL_GROUP + j
            i, k = ids_s[0, b], ids_s[1, b]
            x = shares_of(scores[b], cb[k], ub[i])
            ready[b] = x.reshape(BLK, BLK).astype(jnp.bfloat16)
        piece(g).start()

    for g in range(groups):
        piece(g).wait()


def in_hbm(array):
    return pltpu.with_memory_space_constraint(array, pltpu.HBM)


def on_device(n_user, n_camp, user_emb, camp_emb, block_ids, spend_caps):
    user_count, camp_count = user_emb.shape[0], camp_emb.shape[0]
    feature_dim = user_emb.shape[1] * n_camp
    user_blocks, camp_blocks = user_count // BLK, camp_count // BLK
    ids = block_ids.reshape(-1, 2).T
    blocks = ids.shape[1]
    pairs_camp = blocks * n_user * BLK * BLK // camp_count
    pairs_user = blocks * n_camp * BLK * BLK // user_count
    caps = spend_caps.reshape(camp_blocks, BLK)
    vmem = pl.BlockSpec(memory_space=pltpu.VMEM)
    hbm = pl.BlockSpec(memory_space=pltpu.HBM)
    dma = pltpu.SemaphoreType.DMA
    x_size, y_size = n_camp // Z_SIZE, n_user // CORES

    def gather_sems(outer, inner):
        return [
            dma,
            dma((max(outer - 1, 1), CHUNKS)), dma((max(outer - 1, 1), CHUNKS)),
            dma((outer, max(inner - 1, 1), CHUNKS)), dma((outer, max(inner - 1, 1), CHUNKS)),
        ]

    scores, user_table, camp_table, camp_duals, user_duals = pl.pallas_call(
        functools.partial(
            ascent, n_user, n_camp, 1.0 / math.sqrt(feature_dim), pairs_camp, pairs_user
        ),
        name="ascent",
        out_shape=(
            jax.ShapeDtypeStruct((blocks, BLK, BLK), jnp.bfloat16),
            jax.ShapeDtypeStruct((user_blocks, BLK, BLK), jnp.float32),
            jax.ShapeDtypeStruct((camp_blocks, 8, BLK), jnp.float32),
            jax.ShapeDtypeStruct((camp_blocks, BLK), jnp.float32),
            jax.ShapeDtypeStruct((user_blocks, BLK), jnp.float32),
        ),
        in_specs=[hbm] * 4,
        out_specs=(vmem,) * 5,
        scratch_shapes=[
            pltpu.VMEM((feature_dim, user_count), jnp.bfloat16),
            pltpu.VMEM((feature_dim, camp_count), jnp.bfloat16),
            pltpu.VMEM((user_count, feature_dim), jnp.bfloat16),
            pltpu.VMEM((user_blocks * camp_blocks, BLK, BLK), jnp.bfloat16),
            pltpu.VMEM((blocks, BLK), jnp.float32),
            pltpu.VMEM((blocks // BLK, BLK, BLK), jnp.float32),
            pltpu.VMEM((STEPS, n_user, camp_blocks, BLK), jnp.float32),
            pltpu.VMEM((STEPS, n_camp, user_blocks, BLK), jnp.float32),
            dma, dma((n_camp, CHUNKS)), dma((max(x_size - 1, 1), CHUNKS)), dma((x_size, 2, CHUNKS)),
            dma((2, x_size, CHUNKS)), dma((3, max(x_size - 1, 1), CHUNKS)),
            *gather_sems(y_size, CORES),
            dma((STEPS, n_user - 1)), dma((STEPS, n_user - 1)),
            dma((STEPS, n_camp - 1)), dma((STEPS, n_camp - 1)),
            pltpu.SMEM((2, blocks), jnp.int32),
            pltpu.VMEM((2, blocks), jnp.int32),
            pltpu.VMEM((camp_blocks, BLK), jnp.int32),
            dma((3,)),
        ],
        compiler_params=pltpu.CompilerParams(
            collective_id=0, has_side_effects=True, vmem_limit_bytes=43 * 2**20
        ),
    )(in_hbm(user_emb.T), in_hbm(camp_emb.T), in_hbm(ids), in_hbm(caps))

    allocation, camp_duals, user_duals = pl.pallas_call(
        final,
        name="final",
        out_shape=(
            jax.ShapeDtypeStruct((blocks, BLK, BLK), jnp.bfloat16),
            jax.ShapeDtypeStruct((camp_blocks, BLK), jnp.float32),
            jax.ShapeDtypeStruct((user_blocks, BLK), jnp.float32),
        ),
        in_specs=[pl.BlockSpec(memory_space=pltpu.SMEM)] + [vmem] * 5,
        out_specs=(hbm, vmem, vmem),
        scratch_shapes=[
            pltpu.VMEM((blocks, BLK, BLK), jnp.bfloat16),
            dma((blocks // FINAL_GROUP,)),
        ],
        compiler_params=pltpu.CompilerParams(vmem_limit_bytes=14 * 2**20),
    )(in_hbm(ids), scores, user_table, camp_table, camp_duals, user_duals)
    return (
        allocation.reshape(1, 1, blocks, BLK, BLK),
        camp_duals.reshape(-1),
        user_duals.reshape(-1),
    )


def solution(mesh):
    placed = (P("user", "camp"), P("camp", "user"), P("user", "camp", None, None), P("camp"))
    return jax.shard_map(
        functools.partial(on_device, mesh.shape["user"], mesh.shape["camp"]),
        mesh=mesh,
        in_specs=placed,
        out_specs=(P("user", "camp", None, None, None), P("camp"), P("user")),
        check_vma=False,
    )
```

```python
import functools
import math

import jax
import jax.numpy as jnp
from jax import lax
from jax.experimental import pallas as pl
from jax.experimental.pallas import tpu as pltpu
from jax.sharding import PartitionSpec as P

STEPS = 3
step_size = 2.0
user_quota = 0.25
BLK = 128
Z_SIZE = 4
CORES = 2
CHUNKS = 8
AHEAD = 5
EARLY = 1
FINAL_GROUP = 16
MESH = pl.DeviceIdType.MESH


def remote(src, dst, send_sem, recv_sem, axis, target):
    return pltpu.make_async_remote_copy(
        src_ref=src,
        dst_ref=dst,
        send_sem=send_sem,
        recv_sem=recv_sem,
        device_id={axis: target},
        device_id_type=MESH,
    )


class Gather:
    def __init__(self, axis, outer_n, inner_n, src, full, sems):
        self.axis, self.outer_n, self.inner_n = axis, outer_n, inner_n
        self.src, self.full = src, full
        self.own_sem, self.o_send, self.o_recv, self.i_send, self.i_recv = sems
        self.me = lax.axis_index(axis)
        self.o = lax.div(self.me, inner_n)
        self.i = lax.rem(self.me, inner_n)
        self.rows = src.shape[0]
        self.width = src.shape[1] // CHUNKS

    def piece(self, owner, c):
        start = pl.multiple_of(owner * self.rows, self.rows)
        return self.full.at[pl.ds(start, self.rows), pl.ds(c * self.width, self.width)]

    def mine(self, c):
        return self.src.at[:, pl.ds(c * self.width, self.width)]

    def own_copy(self):
        start = pl.multiple_of(self.me * self.rows, self.rows)
        return pltpu.make_async_copy(
            self.src, self.full.at[pl.ds(start, self.rows), :], self.own_sem
        )

    def outer_copy(self, d, c):
        target = lax.rem(self.o + d, self.outer_n) * self.inner_n + self.i
        return remote(
            self.mine(c), self.piece(self.me, c),
            self.o_send.at[d - 1, c], self.o_recv.at[d - 1, c], self.axis, target,
        )

    def inner_copy(self, d, e, c):
        owner = lax.rem(self.o - d + self.outer_n, self.outer_n) * self.inner_n + self.i
        target = self.o * self.inner_n + lax.rem(self.i + e, self.inner_n)
        src = self.mine(c) if d == 0 else self.piece(owner, c)
        return remote(
            src, self.piece(owner, c),
            self.i_send.at[d, e - 1, c], self.i_recv.at[d, e - 1, c], self.axis, target,
        )

    def begin(self, c):
        for d in range(1, self.outer_n):
            self.outer_copy(d, c).start()
        for e in range(1, self.inner_n):
            self.inner_copy(0, e, c).start()

    def forward(self, c):
        for d in range(1, self.outer_n):
            self.outer_copy(d, c).wait_recv()
            for e in range(1, self.inner_n):
                self.inner_copy(d, e, c).start()

    def finish_recv(self, c):
        for d in range(self.outer_n):
            for e in range(1, self.inner_n):
                self.inner_copy(d, e, c).wait_recv()

    def finish_send(self):
        for c in range(CHUNKS):
            for d in range(1, self.outer_n):
                self.outer_copy(d, c).wait_send()
            for d in range(self.outer_n):
                for e in range(1, self.inner_n):
                    self.inner_copy(d, e, c).wait_send()


class Plane:
    def __init__(self, axis, across, src, full, sems):
        self.axis, self.across, self.src, self.full = axis, across, src, full
        self.own_sem, self.arrived, self.x_own, self.z_own, self.z_on, self.x_on = sems
        self.me = lax.axis_index(axis)
        self.z, self.x = lax.div(self.me, across), lax.rem(self.me, across)
        self.pair = self.z + 1 - 2 * lax.rem(self.z, 2)
        self.other = jnp.where(self.z < 2, 2, 1)
        self.far = jnp.where(self.z < 2, 2, 0)
        self.inner = (self.z == 1) | (self.z == 2)
        self.rows = src.shape[0]
        self.width = src.shape[1] // CHUNKS

    def at(self, z, e=0):
        return z * self.across + lax.rem(self.x + e, self.across)

    def columns(self, c):
        return pl.ds(pl.multiple_of(c * self.width, self.width), self.width)

    def piece(self, owner, c):
        start = pl.multiple_of(owner * self.rows, self.rows)
        return self.full.at[pl.ds(start, self.rows), self.columns(c)]

    def own_copy(self):
        start = pl.multiple_of(self.me * self.rows, self.rows)
        return pltpu.make_async_copy(
            self.src, self.full.at[pl.ds(start, self.rows), :], self.own_sem
        )

    def copy(self, owner, c, sem, target, own=False):
        src = self.src.at[:, self.columns(c)] if own else self.piece(owner, c)
        return remote(
            src, self.piece(owner, c), sem, self.arrived.at[owner, c], self.axis, target
        )

    def wait(self, owner, c):
        self.copy(owner, c, self.x_own.at[0, 0], self.at(self.pair)).wait_recv()

    def across_own(self, c):
        return [
            self.copy(self.me, c, self.x_own.at[e - 1, c], self.at(self.z, e), True)
            for e in range(1, self.across)
        ]

    def along_own(self, c, e=0):
        owner = self.at(self.z, e)
        return [
            self.copy(owner, c, self.z_own.at[e, n, c], self.at(z), e == 0)
            for n, z in enumerate((self.pair, self.other))
        ]

    def along_on(self, c, e=0):
        return [
            self.copy(self.at(self.far + n, e), c, self.z_on.at[n, e, c], self.at(self.pair))
            for n in range(2)
        ]

    def across_on(self, c, which):
        zs = (self.pair,) if which == 0 else (self.far, self.far + 1)
        return [
            self.copy(self.at(z), c, self.x_on.at[which + n, e - 1, c], self.at(self.z, e))
            for n, z in enumerate(zs)
            for e in range(1, self.across)
        ]

    def pass_along(self, c, e=0):
        @pl.when(self.inner)
        def _():
            for n, copy in enumerate(self.along_on(c, e)):
                self.wait(self.at(self.far + n, e), c)
                copy.start()

    def pass_along_last(self, c):
        for e in range(1, self.across):
            self.wait(self.at(self.z, e), c)
            start_all(self.along_own(c, e))
        for e in range(self.across):
            self.pass_along(c, e)

    def pass_across_pair(self, c):
        self.wait(self.at(self.pair), c)
        start_all(self.across_on(c, 0))

    def wait_far(self, c, e=0):
        @pl.when(jnp.logical_not(self.inner))
        def _():
            for n in range(2):
                self.wait(self.at(self.far + n, e), c)

    def pass_across_far(self, c):
        self.wait_far(c)
        start_all(self.across_on(c, 1))

    def finish(self, c):
        for e in range(1, self.across):
            for z in (self.z, self.pair, self.far, self.far + 1):
                self.wait(self.at(z, e), c)

    def finish_last(self, c):
        for e in range(self.across):
            self.wait(self.at(self.pair, e), c)
            self.wait_far(c, e)

    def finish_send(self):
        @pl.loop(0, CHUNKS)
        def _(c):
            sent_all(self.across_own(c))
            sent_all(self.along_own(c))

            @pl.when(self.inner)
            def _():
                sent_all(self.along_on(c))

            @pl.when(c < CHUNKS - 1)
            def _():
                sent_all(self.across_on(c, 0))
                sent_all(self.across_on(c, 1))

        for e in range(1, self.across):
            sent_all(self.along_own(CHUNKS - 1, e))

            @pl.when(self.inner)
            def _(e=e):
                sent_all(self.along_on(CHUNKS - 1, e))


def start_all(copies):
    for copy in copies:
        copy.start()


def sent_all(copies):
    for copy in copies:
        copy.wait_send()


def spread_users(table, ub):
    columns = table.T
    for i in range(table.shape[0]):
        ub[i] = jnp.broadcast_to(columns[:, i : i + 1], (BLK, BLK))


def spread_camps(table, cb):
    for i in range(table.shape[0]):
        cb[i] = jnp.broadcast_to(table[i : i + 1, :], (8, BLK))


def shares_of(tile, camp_part, user_part):
    x = tile.astype(jnp.float32).reshape(BLK // 8, 8, BLK)
    x = x - camp_part[None] - user_part.reshape(BLK // 8, 8, BLK)
    return jnp.clip(x, 0.0, 1.0)


def parts_of(values):
    high = values.astype(jnp.bfloat16)
    return high, (values - high.astype(jnp.float32)).astype(jnp.bfloat16)


def ascent(
    n_user, n_camp, score_scale, pairs_camp, pairs_user,
    ut, ct, ids_hbm, caps_hbm,
    sc, ub, cb, camp_out, user_out,
    uf, cf, un, dense, colsum, rowsum, spend_slots, load_slots,
    u_own, u_arrived, u_xown, u_zown, u_zon, u_xon,
    c_own, c_osend, c_orecv, c_isend, c_irecv,
    s_send, s_recv, l_send, l_recv,
    ids_s, ids_v, caps, small_sem,
):
    me_camp, me_user = lax.axis_index("camp"), lax.axis_index("user")
    blocks = ids_s.shape[1]
    user_blocks, camp_blocks = ub.shape[0], cb.shape[0]

    users = Plane(
        "camp", n_camp // Z_SIZE, ut, uf, (u_own, u_arrived, u_xown, u_zown, u_zon, u_xon)
    )
    camps = Gather("user", n_user // CORES, CORES, ct, cf, (c_own, c_osend, c_orecv, c_isend, c_irecv))
    small = [
        pltpu.make_async_copy(ids_hbm, ids_s, small_sem.at[0]),
        pltpu.make_async_copy(ids_hbm, ids_v, small_sem.at[1]),
        pltpu.make_async_copy(caps_hbm, caps, small_sem.at[2]),
    ]
    for copy in small:
        copy.start()
    users.own_copy().start()
    camps.own_copy().start()

    barrier = pltpu.get_barrier_semaphore()
    for d in range(1, n_camp):
        pl.semaphore_signal(
            barrier, inc=1, device_id={"camp": lax.rem(me_camp + d, n_camp)}, device_id_type=MESH
        )
    for d in range(1, n_user):
        pl.semaphore_signal(
            barrier, inc=1, device_id={"user": lax.rem(me_user + d, n_user)}, device_id_type=MESH
        )
    pl.semaphore_wait(barrier, n_camp + n_user - 2)

    for c in range(CHUNKS):
        start_all(users.across_own(c))
        if c < AHEAD:
            start_all(users.along_own(c))
        camps.begin(c)

    columns = uf.shape[1] // CHUNKS
    wide = cf.shape[1] // 2

    def turn(c):
        at = pl.ds(pl.multiple_of(c * columns, columns), columns)
        un[at, :] = uf[:, at].astype(jnp.float32).T.astype(jnp.bfloat16)

    def multiply(c, side):
        right = cf[:, side * wide : (side + 1) * wide]
        for r in range(columns // BLK):
            rows = pl.ds(pl.multiple_of(c * columns + r * BLK, BLK), BLK)
            product = jnp.dot(un[rows, :], right, preferred_element_type=jnp.float32)
            tiles = (product * score_scale).astype(jnp.bfloat16)
            first = (c * (columns // BLK) + r) * camp_blocks + side * (wide // BLK)
            for k in range(wide // BLK):
                dense[first + k] = tiles[:, k * BLK : (k + 1) * BLK]

    def pass_on(c):
        users.pass_along(c)
        start_all(users.along_own(c + AHEAD))

    last = CHUNKS - 1

    def arrive(t):
        @pl.when(t + 2 < last)
        def _():
            users.pass_across_far(t + 2)

        @pl.when(t + 4 < last)
        def _():
            users.pass_along(t + 4)
            users.pass_across_pair(t + 4)

        @pl.when(t + 4 == last)
        def _():
            users.pass_along_last(last)

        c = jnp.where(t < last - 1, t, 2 * last - 1 - t)

        @pl.when(c < last)
        def _():
            users.finish(c)

        @pl.when(c == last)
        def _():
            users.finish_last(last)

        turn(c)
        return c

    half = CHUNKS // 2
    pass_on(0)
    camps.forward(0)
    users.pass_across_pair(0)
    users.pass_across_pair(1)
    camps.forward(1)
    pass_on(1)
    camps.forward(2)
    users.pass_across_pair(2)
    pass_on(2)
    users.pass_across_far(0)
    camps.forward(3)
    users.pass_across_pair(3)
    users.pass_along(3)
    users.pass_across_far(1)
    users.own_copy().wait()
    camps.own_copy().wait()
    for c in range(half):
        camps.finish_recv(c)

    @pl.loop(0, EARLY)
    def _(c):
        camps.forward(half + c)
        arrive(c)
        multiply(c, 0)

    for c in range(half + EARLY, CHUNKS):
        camps.forward(c)
    for c in range(half, CHUNKS):
        camps.finish_recv(c)

    @pl.loop(0, EARLY)
    def _(c):
        multiply(c, 1)

    @pl.loop(EARLY, CHUNKS)
    def _(c):
        c = arrive(c)
        multiply(c, 0)
        multiply(c, 1)

    lanes = lax.broadcasted_iota(jnp.int32, (BLK // 8, 8, BLK), 2)
    for copy in small:
        copy.wait()
    ids_rows = ids_v[0:1, :]
    ids_cols = ids_v[1:2, :]
    user_hits = jnp.where(
        lax.broadcasted_iota(jnp.int32, (user_blocks, blocks), 0) == ids_rows, 1.0, 0.0
    ).astype(jnp.bfloat16)
    camp_hits = jnp.where(
        lax.broadcasted_iota(jnp.int32, (camp_blocks, blocks), 0) == ids_cols, 1.0, 0.0
    ).astype(jnp.bfloat16)
    cap_float = caps[...].astype(jnp.float32)
    camp_duals = jnp.zeros((camp_blocks, BLK), jnp.float32)
    user_duals = jnp.zeros((user_blocks, BLK), jnp.float32)

    ones = jnp.where(
        lax.broadcasted_iota(jnp.int32, (2 * BLK, BLK), 0) // BLK
        == lax.broadcasted_iota(jnp.int32, (2 * BLK, BLK), 1) % 2, 1.0, 0.0,
    )

    def half_sums(half, first):
        sums = jnp.zeros((BLK // 8, 8, BLK), jnp.float32)
        for p in range(BLK // 2):
            pair = []
            for j in (2 * p, 2 * p + 1):
                b = half * BLK + j
                i, k = ids_s[0, b], ids_s[1, b]
                if first:
                    tile = dense[i * camp_blocks + k]
                    sc[b] = tile
                    x = jnp.clip(tile.astype(jnp.float32), 0.0, 1.0).reshape(BLK // 8, 8, BLK)
                else:
                    x = shares_of(sc[b], cb[k], ub[i])
                colsum[pl.ds(b, 1), :] = jnp.sum(jnp.sum(x, axis=0), axis=0, keepdims=True)
                if p % 2:
                    sums = jnp.where(lanes == j, jnp.sum(x, axis=2, keepdims=True), sums)
                pair.append(x.reshape(BLK, BLK))
            if p % 2 == 0:
                both = jnp.dot(
                    jnp.concatenate(pair, axis=1), ones, preferred_element_type=jnp.float32
                )
                sums = jnp.where(lanes // 2 == p, both.reshape(BLK // 8, 8, BLK), sums)
        rowsum[half] = sums.reshape(BLK, BLK)

    def step(sweep, duals, first):
        camp_duals, user_duals = duals

        @pl.loop(0, blocks // BLK)
        def _(half):
            half_sums(half, first)

        load = 0.0
        for half in range(blocks // BLK):
            hits = user_hits[:, half * BLK : (half + 1) * BLK]
            load = load + lax.dot_general(
                jnp.concatenate([hits, hits], axis=1),
                jnp.concatenate(parts_of(rowsum[half]), axis=1),
                (((1,), (1,)), ((), ())), preferred_element_type=jnp.float32,
            )
        load_slots[sweep, me_camp] = load
        load_copies = []
        for d in range(1, n_camp):
            slot = load_slots.at[sweep, me_camp]
            load_copies.append(remote(
                slot, slot, l_send.at[sweep, d - 1], l_recv.at[sweep, d - 1],
                "camp", lax.rem(me_camp + d, n_camp),
            ))
            load_copies[-1].start()
        spend = jnp.dot(
            jnp.concatenate([camp_hits, camp_hits], axis=1),
            jnp.concatenate(parts_of(colsum[...]), axis=0), preferred_element_type=jnp.float32,
        )
        spend_slots[sweep, me_user] = spend
        spend_copies = []
        for d in range(1, n_user):
            slot = spend_slots.at[sweep, me_user]
            spend_copies.append(remote(
                slot, slot, s_send.at[sweep, d - 1], s_recv.at[sweep, d - 1],
                "user", lax.rem(me_user + d, n_user),
            ))
            spend_copies[-1].start()
        for copy in spend_copies:
            copy.wait_recv()
        spend = spend_slots[sweep, 0]
        for k in range(1, n_user):
            spend = spend + spend_slots[sweep, k]
        camp_duals = jnp.maximum(
            0.0, camp_duals + step_size * (spend - cap_float) / pairs_camp
        )
        spread_camps(camp_duals, cb)
        for copy in load_copies:
            copy.wait_recv()
        load = load_slots[sweep, 0]
        for k in range(1, n_camp):
            load = load + load_slots[sweep, k]
        user_duals = jnp.maximum(
            0.0, user_duals + step_size * (load - user_quota * pairs_user) / pairs_user
        )
        spread_users(user_duals, ub)
        for copy in load_copies + spend_copies:
            copy.wait_send()
        return camp_duals, user_duals

    duals = step(0, (camp_duals, user_duals), True)
    camp_duals, user_duals = lax.fori_loop(1, STEPS, lambda n, d: step(n, d, False), duals)

    camp_out[...] = camp_duals
    user_out[...] = user_duals
    users.finish_send()
    camps.finish_send()


def final(ids_s, scores, ub, cb, camp_duals, user_duals, alloc, camp_out, user_out, ready, sems):
    camp_out[...] = camp_duals[...]
    user_out[...] = user_duals[...]
    groups = scores.shape[0] // FINAL_GROUP

    def piece(g):
        at = pl.ds(pl.multiple_of(g * FINAL_GROUP, FINAL_GROUP), FINAL_GROUP)
        return pltpu.make_async_copy(ready.at[at], alloc.at[at], sems.at[g])

    @pl.loop(0, groups)
    def _(g):
        for j in range(FINAL_GROUP):
            b = g * FINAL_GROUP + j
            i, k = ids_s[0, b], ids_s[1, b]
            x = shares_of(scores[b], cb[k], ub[i])
            ready[b] = x.reshape(BLK, BLK).astype(jnp.bfloat16)
        piece(g).start()

    for g in range(groups):
        piece(g).wait()


def in_hbm(array):
    return pltpu.with_memory_space_constraint(array, pltpu.HBM)


def on_device(n_user, n_camp, user_emb, camp_emb, block_ids, spend_caps):
    user_count, camp_count = user_emb.shape[0], camp_emb.shape[0]
    feature_dim = user_emb.shape[1] * n_camp
    user_blocks, camp_blocks = user_count // BLK, camp_count // BLK
    ids = block_ids.reshape(-1, 2).T
    blocks = ids.shape[1]
    pairs_camp = blocks * n_user * BLK * BLK // camp_count
    pairs_user = blocks * n_camp * BLK * BLK // user_count
    caps = spend_caps.reshape(camp_blocks, BLK)
    vmem = pl.BlockSpec(memory_space=pltpu.VMEM)
    hbm = pl.BlockSpec(memory_space=pltpu.HBM)
    dma = pltpu.SemaphoreType.DMA
    x_size, y_size = n_camp // Z_SIZE, n_user // CORES

    def gather_sems(outer, inner):
        return [
            dma,
            dma((max(outer - 1, 1), CHUNKS)), dma((max(outer - 1, 1), CHUNKS)),
            dma((outer, max(inner - 1, 1), CHUNKS)), dma((outer, max(inner - 1, 1), CHUNKS)),
        ]

    scores, user_table, camp_table, camp_duals, user_duals = pl.pallas_call(
        functools.partial(
            ascent, n_user, n_camp, 1.0 / math.sqrt(feature_dim), pairs_camp, pairs_user
        ),
        name="ascent",
        out_shape=(
            jax.ShapeDtypeStruct((blocks, BLK, BLK), jnp.bfloat16),
            jax.ShapeDtypeStruct((user_blocks, BLK, BLK), jnp.float32),
            jax.ShapeDtypeStruct((camp_blocks, 8, BLK), jnp.float32),
            jax.ShapeDtypeStruct((camp_blocks, BLK), jnp.float32),
            jax.ShapeDtypeStruct((user_blocks, BLK), jnp.float32),
        ),
        in_specs=[hbm] * 4,
        out_specs=(vmem,) * 5,
        scratch_shapes=[
            pltpu.VMEM((feature_dim, user_count), jnp.bfloat16),
            pltpu.VMEM((feature_dim, camp_count), jnp.bfloat16),
            pltpu.VMEM((user_count, feature_dim), jnp.bfloat16),
            pltpu.VMEM((user_blocks * camp_blocks, BLK, BLK), jnp.bfloat16),
            pltpu.VMEM((blocks, BLK), jnp.float32),
            pltpu.VMEM((blocks // BLK, BLK, BLK), jnp.float32),
            pltpu.VMEM((STEPS, n_user, camp_blocks, BLK), jnp.float32),
            pltpu.VMEM((STEPS, n_camp, user_blocks, BLK), jnp.float32),
            dma, dma((n_camp, CHUNKS)), dma((max(x_size - 1, 1), CHUNKS)), dma((x_size, 2, CHUNKS)),
            dma((2, x_size, CHUNKS)), dma((3, max(x_size - 1, 1), CHUNKS)),
            *gather_sems(y_size, CORES),
            dma((STEPS, n_user - 1)), dma((STEPS, n_user - 1)),
            dma((STEPS, n_camp - 1)), dma((STEPS, n_camp - 1)),
            pltpu.SMEM((2, blocks), jnp.int32),
            pltpu.VMEM((2, blocks), jnp.int32),
            pltpu.VMEM((camp_blocks, BLK), jnp.int32),
            dma((3,)),
        ],
        compiler_params=pltpu.CompilerParams(
            collective_id=0, has_side_effects=True, vmem_limit_bytes=43 * 2**20
        ),
    )(in_hbm(user_emb.T), in_hbm(camp_emb.T), in_hbm(ids), in_hbm(caps))

    allocation, camp_duals, user_duals = pl.pallas_call(
        final,
        name="final",
        out_shape=(
            jax.ShapeDtypeStruct((blocks, BLK, BLK), jnp.bfloat16),
            jax.ShapeDtypeStruct((camp_blocks, BLK), jnp.float32),
            jax.ShapeDtypeStruct((user_blocks, BLK), jnp.float32),
        ),
        in_specs=[pl.BlockSpec(memory_space=pltpu.SMEM)] + [vmem] * 5,
        out_specs=(hbm, vmem, vmem),
        scratch_shapes=[
            pltpu.VMEM((blocks, BLK, BLK), jnp.bfloat16),
            dma((blocks // FINAL_GROUP,)),
        ],
        compiler_params=pltpu.CompilerParams(vmem_limit_bytes=14 * 2**20),
    )(in_hbm(ids), scores, user_table, camp_table, camp_duals, user_duals)
    return (
        allocation.reshape(1, 1, blocks, BLK, BLK),
        camp_duals.reshape(-1),
        user_duals.reshape(-1),
    )


def solution(mesh):
    placed = (P("user", "camp"), P("camp", "user"), P("user", "camp", None, None), P("camp"))
    return jax.shard_map(
        functools.partial(on_device, mesh.shape["user"], mesh.shape["camp"]),
        mesh=mesh,
        in_specs=placed,
        out_specs=(P("user", "camp", None, None, None), P("camp"), P("user")),
        check_vma=False,
    )
```

```python
import functools
import math

import jax
import jax.numpy as jnp
from jax import lax
from jax.experimental import pallas as pl
from jax.experimental.pallas import tpu as pltpu
from jax.sharding import PartitionSpec as P

STEPS = 3
step_size = 2.0
user_quota = 0.25
BLK = 128
Z_SIZE = 4
CORES = 2
CHUNKS = 8
AHEAD = 5
EARLY = 1
FINAL_GROUP = 16
MESH = pl.DeviceIdType.MESH


def remote(src, dst, send_sem, recv_sem, axis, target):
    return pltpu.make_async_remote_copy(
        src_ref=src,
        dst_ref=dst,
        send_sem=send_sem,
        recv_sem=recv_sem,
        device_id={axis: target},
        device_id_type=MESH,
    )


class Gather:
    def __init__(self, axis, outer_n, inner_n, src, full, sems):
        self.axis, self.outer_n, self.inner_n = axis, outer_n, inner_n
        self.src, self.full = src, full
        self.own_sem, self.o_send, self.o_recv, self.i_send, self.i_recv = sems
        self.me = lax.axis_index(axis)
        self.o = lax.div(self.me, inner_n)
        self.i = lax.rem(self.me, inner_n)
        self.rows = src.shape[0]
        self.width = src.shape[1] // CHUNKS

    def piece(self, owner, c):
        start = pl.multiple_of(owner * self.rows, self.rows)
        return self.full.at[pl.ds(start, self.rows), pl.ds(c * self.width, self.width)]

    def mine(self, c):
        return self.src.at[:, pl.ds(c * self.width, self.width)]

    def own_copy(self):
        start = pl.multiple_of(self.me * self.rows, self.rows)
        return pltpu.make_async_copy(
            self.src, self.full.at[pl.ds(start, self.rows), :], self.own_sem
        )

    def outer_copy(self, d, c):
        target = lax.rem(self.o + d, self.outer_n) * self.inner_n + self.i
        return remote(
            self.mine(c), self.piece(self.me, c),
            self.o_send.at[d - 1, c], self.o_recv.at[d - 1, c], self.axis, target,
        )

    def inner_copy(self, d, e, c):
        owner = lax.rem(self.o - d + self.outer_n, self.outer_n) * self.inner_n + self.i
        target = self.o * self.inner_n + lax.rem(self.i + e, self.inner_n)
        src = self.mine(c) if d == 0 else self.piece(owner, c)
        return remote(
            src, self.piece(owner, c),
            self.i_send.at[d, e - 1, c], self.i_recv.at[d, e - 1, c], self.axis, target,
        )

    def begin(self, c):
        for d in range(1, self.outer_n):
            self.outer_copy(d, c).start()
        for e in range(1, self.inner_n):
            self.inner_copy(0, e, c).start()

    def forward(self, c):
        for d in range(1, self.outer_n):
            self.outer_copy(d, c).wait_recv()
            for e in range(1, self.inner_n):
                self.inner_copy(d, e, c).start()

    def finish_recv(self, c):
        for d in range(self.outer_n):
            for e in range(1, self.inner_n):
                self.inner_copy(d, e, c).wait_recv()

    def finish_send(self):
        for c in range(CHUNKS):
            for d in range(1, self.outer_n):
                self.outer_copy(d, c).wait_send()
            for d in range(self.outer_n):
                for e in range(1, self.inner_n):
                    self.inner_copy(d, e, c).wait_send()


class Plane:
    def __init__(self, axis, across, src, full, sems):
        self.axis, self.across, self.src, self.full = axis, across, src, full
        self.own_sem, self.arrived, self.x_own, self.z_own, self.z_on, self.x_on = sems
        self.me = lax.axis_index(axis)
        self.z, self.x = lax.div(self.me, across), lax.rem(self.me, across)
        self.pair = self.z + 1 - 2 * lax.rem(self.z, 2)
        self.other = jnp.where(self.z < 2, 2, 1)
        self.far = jnp.where(self.z < 2, 2, 0)
        self.inner = (self.z == 1) | (self.z == 2)
        self.rows = src.shape[0]
        self.width = src.shape[1] // CHUNKS

    def at(self, z, e=0):
        return z * self.across + lax.rem(self.x + e, self.across)

    def columns(self, c):
        return pl.ds(pl.multiple_of(c * self.width, self.width), self.width)

    def piece(self, owner, c):
        start = pl.multiple_of(owner * self.rows, self.rows)
        return self.full.at[pl.ds(start, self.rows), self.columns(c)]

    def own_copy(self):
        start = pl.multiple_of(self.me * self.rows, self.rows)
        return pltpu.make_async_copy(
            self.src, self.full.at[pl.ds(start, self.rows), :], self.own_sem
        )

    def copy(self, owner, c, sem, target, own=False):
        src = self.src.at[:, self.columns(c)] if own else self.piece(owner, c)
        return remote(
            src, self.piece(owner, c), sem, self.arrived.at[owner, c], self.axis, target
        )

    def wait(self, owner, c):
        self.copy(owner, c, self.x_own.at[0, 0], self.at(self.pair)).wait_recv()

    def across_own(self, c):
        return [
            self.copy(self.me, c, self.x_own.at[e - 1, c], self.at(self.z, e), True)
            for e in range(1, self.across)
        ]

    def along_own(self, c, e=0):
        owner = self.at(self.z, e)
        return [
            self.copy(owner, c, self.z_own.at[e, n, c], self.at(z), e == 0)
            for n, z in enumerate((self.pair, self.other))
        ]

    def along_on(self, c, e=0):
        return [
            self.copy(self.at(self.far + n, e), c, self.z_on.at[n, e, c], self.at(self.pair))
            for n in range(2)
        ]

    def across_on(self, c, which):
        zs = (self.pair,) if which == 0 else (self.far, self.far + 1)
        return [
            self.copy(self.at(z), c, self.x_on.at[which + n, e - 1, c], self.at(self.z, e))
            for n, z in enumerate(zs)
            for e in range(1, self.across)
        ]

    def pass_along(self, c, e=0):
        @pl.when(self.inner)
        def _():
            for n, copy in enumerate(self.along_on(c, e)):
                self.wait(self.at(self.far + n, e), c)
                copy.start()

    def pass_along_last(self, c):
        for e in range(1, self.across):
            self.wait(self.at(self.z, e), c)
            start_all(self.along_own(c, e))
        for e in range(self.across):
            self.pass_along(c, e)

    def pass_across_pair(self, c):
        self.wait(self.at(self.pair), c)
        start_all(self.across_on(c, 0))

    def wait_far(self, c, e=0):
        @pl.when(jnp.logical_not(self.inner))
        def _():
            for n in range(2):
                self.wait(self.at(self.far + n, e), c)

    def pass_across_far(self, c):
        self.wait_far(c)
        start_all(self.across_on(c, 1))

    def finish(self, c):
        for e in range(1, self.across):
            for z in (self.z, self.pair, self.far, self.far + 1):
                self.wait(self.at(z, e), c)

    def finish_last(self, c):
        for e in range(self.across):
            self.wait(self.at(self.pair, e), c)
            self.wait_far(c, e)

    def finish_send(self):
        @pl.loop(0, CHUNKS)
        def _(c):
            sent_all(self.across_own(c))
            sent_all(self.along_own(c))

            @pl.when(self.inner)
            def _():
                sent_all(self.along_on(c))

            @pl.when(c < CHUNKS - 1)
            def _():
                sent_all(self.across_on(c, 0))
                sent_all(self.across_on(c, 1))

        for e in range(1, self.across):
            sent_all(self.along_own(CHUNKS - 1, e))

            @pl.when(self.inner)
            def _(e=e):
                sent_all(self.along_on(CHUNKS - 1, e))


def start_all(copies):
    for copy in copies:
        copy.start()


def sent_all(copies):
    for copy in copies:
        copy.wait_send()


def spread_users(table, ub):
    columns = table.T
    for i in range(table.shape[0]):
        ub[i] = jnp.broadcast_to(columns[:, i : i + 1], (BLK, BLK))


def spread_camps(table, cb):
    for i in range(table.shape[0]):
        cb[i] = jnp.broadcast_to(table[i : i + 1, :], (8, BLK))


def shares_of(tile, camp_part, user_part):
    x = tile.astype(jnp.float32).reshape(BLK // 8, 8, BLK)
    x = x - camp_part[None] - user_part.reshape(BLK // 8, 8, BLK)
    return jnp.clip(x, 0.0, 1.0)


def parts_of(values):
    high = values.astype(jnp.bfloat16)
    return high, (values - high.astype(jnp.float32)).astype(jnp.bfloat16)


def ascent(
    n_user, n_camp, score_scale, pairs_camp, pairs_user,
    ut, ct, ids_hbm, caps_hbm,
    sc, ub, cb, camp_out, user_out,
    uf, cf, un, dense, colsum, rowsum, spend_slots, load_slots,
    u_own, u_arrived, u_xown, u_zown, u_zon, u_xon,
    c_own, c_osend, c_orecv, c_isend, c_irecv,
    s_send, s_recv, l_send, l_recv,
    ids_s, ids_v, caps, small_sem,
):
    me_camp, me_user = lax.axis_index("camp"), lax.axis_index("user")
    blocks = ids_s.shape[1]
    user_blocks, camp_blocks = ub.shape[0], cb.shape[0]

    users = Plane(
        "camp", n_camp // Z_SIZE, ut, uf, (u_own, u_arrived, u_xown, u_zown, u_zon, u_xon)
    )
    camps = Gather("user", n_user // CORES, CORES, ct, cf, (c_own, c_osend, c_orecv, c_isend, c_irecv))
    small = [
        pltpu.make_async_copy(ids_hbm, ids_s, small_sem.at[0]),
        pltpu.make_async_copy(ids_hbm, ids_v, small_sem.at[1]),
        pltpu.make_async_copy(caps_hbm, caps, small_sem.at[2]),
    ]
    for copy in small:
        copy.start()
    users.own_copy().start()
    camps.own_copy().start()

    barrier = pltpu.get_barrier_semaphore()
    for d in range(1, n_camp):
        pl.semaphore_signal(
            barrier, inc=1, device_id={"camp": lax.rem(me_camp + d, n_camp)}, device_id_type=MESH
        )
    for d in range(1, n_user):
        pl.semaphore_signal(
            barrier, inc=1, device_id={"user": lax.rem(me_user + d, n_user)}, device_id_type=MESH
        )
    pl.semaphore_wait(barrier, n_camp + n_user - 2)

    for c in range(CHUNKS):
        start_all(users.across_own(c))
        if c < AHEAD:
            start_all(users.along_own(c))
        camps.begin(c)

    columns = uf.shape[1] // CHUNKS
    wide = cf.shape[1] // 2

    def turn(c):
        at = pl.ds(pl.multiple_of(c * columns, columns), columns)
        un[at, :] = uf[:, at].astype(jnp.float32).T.astype(jnp.bfloat16)

    def multiply(c, side):
        right = cf[:, side * wide : (side + 1) * wide]
        for r in range(columns // BLK):
            rows = pl.ds(pl.multiple_of(c * columns + r * BLK, BLK), BLK)
            product = jnp.dot(un[rows, :], right, preferred_element_type=jnp.float32)
            tiles = (product * score_scale).astype(jnp.bfloat16)
            first = (c * (columns // BLK) + r) * camp_blocks + side * (wide // BLK)
            for k in range(wide // BLK):
                dense[first + k] = tiles[:, k * BLK : (k + 1) * BLK]

    def pass_on(c):
        users.pass_along(c)
        start_all(users.along_own(c + AHEAD))

    last = CHUNKS - 1

    def arrive(t):
        @pl.when(t + 2 < last)
        def _():
            users.pass_across_far(t + 2)

        @pl.when(t + 3 < last)
        def _():
            users.pass_across_pair(t + 3)

        @pl.when(t + 4 < last)
        def _():
            users.pass_along(t + 4)

        @pl.when(t + 4 == last)
        def _():
            users.pass_along_last(last)

        c = jnp.where(t < last - 1, t, 2 * last - 1 - t)

        @pl.when(c < last)
        def _():
            users.finish(c)

        @pl.when(c == last)
        def _():
            users.finish_last(last)

        turn(c)
        return c

    half = CHUNKS // 2
    pass_on(0)
    camps.forward(0)
    users.pass_across_pair(0)
    users.pass_across_pair(1)
    camps.forward(1)
    pass_on(1)
    camps.forward(2)
    users.pass_across_pair(2)
    pass_on(2)
    users.pass_across_far(0)
    camps.forward(3)
    users.pass_along(3)
    users.pass_across_far(1)
    users.own_copy().wait()
    camps.own_copy().wait()
    for c in range(half):
        camps.finish_recv(c)

    @pl.loop(0, EARLY)
    def _(c):
        camps.forward(half + c)
        arrive(c)
        multiply(c, 0)

    for c in range(half + EARLY, CHUNKS):
        camps.forward(c)
    for c in range(half, CHUNKS):
        camps.finish_recv(c)

    @pl.loop(0, EARLY)
    def _(c):
        multiply(c, 1)

    @pl.loop(EARLY, CHUNKS)
    def _(c):
        c = arrive(c)
        multiply(c, 0)
        multiply(c, 1)

    lanes = lax.broadcasted_iota(jnp.int32, (BLK // 8, 8, BLK), 2)
    for copy in small:
        copy.wait()
    ids_rows = ids_v[0:1, :]
    ids_cols = ids_v[1:2, :]
    user_hits = jnp.where(
        lax.broadcasted_iota(jnp.int32, (user_blocks, blocks), 0) == ids_rows, 1.0, 0.0
    ).astype(jnp.bfloat16)
    camp_hits = jnp.where(
        lax.broadcasted_iota(jnp.int32, (camp_blocks, blocks), 0) == ids_cols, 1.0, 0.0
    ).astype(jnp.bfloat16)
    cap_float = caps[...].astype(jnp.float32)
    camp_duals = jnp.zeros((camp_blocks, BLK), jnp.float32)
    user_duals = jnp.zeros((user_blocks, BLK), jnp.float32)

    ones = jnp.where(
        lax.broadcasted_iota(jnp.int32, (2 * BLK, BLK), 0) // BLK
        == lax.broadcasted_iota(jnp.int32, (2 * BLK, BLK), 1) % 2, 1.0, 0.0,
    )

    def half_sums(half, first):
        sums = jnp.zeros((BLK // 8, 8, BLK), jnp.float32)
        for p in range(BLK // 2):
            pair = []
            for j in (2 * p, 2 * p + 1):
                b = half * BLK + j
                i, k = ids_s[0, b], ids_s[1, b]
                if first:
                    tile = dense[i * camp_blocks + k]
                    sc[b] = tile
                    x = jnp.clip(tile.astype(jnp.float32), 0.0, 1.0).reshape(BLK // 8, 8, BLK)
                else:
                    x = shares_of(sc[b], cb[k], ub[i])
                colsum[pl.ds(b, 1), :] = jnp.sum(jnp.sum(x, axis=0), axis=0, keepdims=True)
                if p % 2:
                    sums = jnp.where(lanes == j, jnp.sum(x, axis=2, keepdims=True), sums)
                pair.append(x.reshape(BLK, BLK))
            if p % 2 == 0:
                both = jnp.dot(
                    jnp.concatenate(pair, axis=1), ones, preferred_element_type=jnp.float32
                )
                sums = jnp.where(lanes // 2 == p, both.reshape(BLK // 8, 8, BLK), sums)
        rowsum[half] = sums.reshape(BLK, BLK)

    def step(sweep, duals, first):
        camp_duals, user_duals = duals

        @pl.loop(0, blocks // BLK)
        def _(half):
            half_sums(half, first)

        load = 0.0
        for half in range(blocks // BLK):
            hits = user_hits[:, half * BLK : (half + 1) * BLK]
            load = load + lax.dot_general(
                jnp.concatenate([hits, hits], axis=1),
                jnp.concatenate(parts_of(rowsum[half]), axis=1),
                (((1,), (1,)), ((), ())), preferred_element_type=jnp.float32,
            )
        load_slots[sweep, me_camp] = load
        load_copies = []
        for d in range(1, n_camp):
            slot = load_slots.at[sweep, me_camp]
            load_copies.append(remote(
                slot, slot, l_send.at[sweep, d - 1], l_recv.at[sweep, d - 1],
                "camp", lax.rem(me_camp + d, n_camp),
            ))
            load_copies[-1].start()
        spend = jnp.dot(
            jnp.concatenate([camp_hits, camp_hits], axis=1),
            jnp.concatenate(parts_of(colsum[...]), axis=0), preferred_element_type=jnp.float32,
        )
        spend_slots[sweep, me_user] = spend
        spend_copies = []
        for d in range(1, n_user):
            slot = spend_slots.at[sweep, me_user]
            spend_copies.append(remote(
                slot, slot, s_send.at[sweep, d - 1], s_recv.at[sweep, d - 1],
                "user", lax.rem(me_user + d, n_user),
            ))
            spend_copies[-1].start()
        for copy in spend_copies:
            copy.wait_recv()
        spend = spend_slots[sweep, 0]
        for k in range(1, n_user):
            spend = spend + spend_slots[sweep, k]
        camp_duals = jnp.maximum(
            0.0, camp_duals + step_size * (spend - cap_float) / pairs_camp
        )
        spread_camps(camp_duals, cb)
        for copy in load_copies:
            copy.wait_recv()
        load = load_slots[sweep, 0]
        for k in range(1, n_camp):
            load = load + load_slots[sweep, k]
        user_duals = jnp.maximum(
            0.0, user_duals + step_size * (load - user_quota * pairs_user) / pairs_user
        )
        spread_users(user_duals, ub)
        for copy in load_copies + spend_copies:
            copy.wait_send()
        return camp_duals, user_duals

    duals = step(0, (camp_duals, user_duals), True)
    camp_duals, user_duals = lax.fori_loop(1, STEPS, lambda n, d: step(n, d, False), duals)

    camp_out[...] = camp_duals
    user_out[...] = user_duals
    users.finish_send()
    camps.finish_send()


def final(ids_s, scores, ub, cb, camp_duals, user_duals, alloc, camp_out, user_out, ready, sems):
    camp_out[...] = camp_duals[...]
    user_out[...] = user_duals[...]
    groups = scores.shape[0] // FINAL_GROUP

    def piece(g):
        at = pl.ds(pl.multiple_of(g * FINAL_GROUP, FINAL_GROUP), FINAL_GROUP)
        return pltpu.make_async_copy(ready.at[at], alloc.at[at], sems.at[g])

    @pl.loop(0, groups)
    def _(g):
        for j in range(FINAL_GROUP):
            b = g * FINAL_GROUP + j
            i, k = ids_s[0, b], ids_s[1, b]
            x = shares_of(scores[b], cb[k], ub[i])
            ready[b] = x.reshape(BLK, BLK).astype(jnp.bfloat16)
        piece(g).start()

    for g in range(groups):
        piece(g).wait()


def in_hbm(array):
    return pltpu.with_memory_space_constraint(array, pltpu.HBM)


def on_device(n_user, n_camp, user_emb, camp_emb, block_ids, spend_caps):
    user_count, camp_count = user_emb.shape[0], camp_emb.shape[0]
    feature_dim = user_emb.shape[1] * n_camp
    user_blocks, camp_blocks = user_count // BLK, camp_count // BLK
    ids = block_ids.reshape(-1, 2).T
    blocks = ids.shape[1]
    pairs_camp = blocks * n_user * BLK * BLK // camp_count
    pairs_user = blocks * n_camp * BLK * BLK // user_count
    caps = spend_caps.reshape(camp_blocks, BLK)
    vmem = pl.BlockSpec(memory_space=pltpu.VMEM)
    hbm = pl.BlockSpec(memory_space=pltpu.HBM)
    dma = pltpu.SemaphoreType.DMA
    x_size, y_size = n_camp // Z_SIZE, n_user // CORES

    def gather_sems(outer, inner):
        return [
            dma,
            dma((max(outer - 1, 1), CHUNKS)), dma((max(outer - 1, 1), CHUNKS)),
            dma((outer, max(inner - 1, 1), CHUNKS)), dma((outer, max(inner - 1, 1), CHUNKS)),
        ]

    scores, user_table, camp_table, camp_duals, user_duals = pl.pallas_call(
        functools.partial(
            ascent, n_user, n_camp, 1.0 / math.sqrt(feature_dim), pairs_camp, pairs_user
        ),
        name="ascent",
        out_shape=(
            jax.ShapeDtypeStruct((blocks, BLK, BLK), jnp.bfloat16),
            jax.ShapeDtypeStruct((user_blocks, BLK, BLK), jnp.float32),
            jax.ShapeDtypeStruct((camp_blocks, 8, BLK), jnp.float32),
            jax.ShapeDtypeStruct((camp_blocks, BLK), jnp.float32),
            jax.ShapeDtypeStruct((user_blocks, BLK), jnp.float32),
        ),
        in_specs=[hbm] * 4,
        out_specs=(vmem,) * 5,
        scratch_shapes=[
            pltpu.VMEM((feature_dim, user_count), jnp.bfloat16),
            pltpu.VMEM((feature_dim, camp_count), jnp.bfloat16),
            pltpu.VMEM((user_count, feature_dim), jnp.bfloat16),
            pltpu.VMEM((user_blocks * camp_blocks, BLK, BLK), jnp.bfloat16),
            pltpu.VMEM((blocks, BLK), jnp.float32),
            pltpu.VMEM((blocks // BLK, BLK, BLK), jnp.float32),
            pltpu.VMEM((STEPS, n_user, camp_blocks, BLK), jnp.float32),
            pltpu.VMEM((STEPS, n_camp, user_blocks, BLK), jnp.float32),
            dma, dma((n_camp, CHUNKS)), dma((max(x_size - 1, 1), CHUNKS)), dma((x_size, 2, CHUNKS)),
            dma((2, x_size, CHUNKS)), dma((3, max(x_size - 1, 1), CHUNKS)),
            *gather_sems(y_size, CORES),
            dma((STEPS, n_user - 1)), dma((STEPS, n_user - 1)),
            dma((STEPS, n_camp - 1)), dma((STEPS, n_camp - 1)),
            pltpu.SMEM((2, blocks), jnp.int32),
            pltpu.VMEM((2, blocks), jnp.int32),
            pltpu.VMEM((camp_blocks, BLK), jnp.int32),
            dma((3,)),
        ],
        compiler_params=pltpu.CompilerParams(
            collective_id=0, has_side_effects=True, vmem_limit_bytes=43 * 2**20
        ),
    )(in_hbm(user_emb.T), in_hbm(camp_emb.T), in_hbm(ids), in_hbm(caps))

    allocation, camp_duals, user_duals = pl.pallas_call(
        final,
        name="final",
        out_shape=(
            jax.ShapeDtypeStruct((blocks, BLK, BLK), jnp.bfloat16),
            jax.ShapeDtypeStruct((camp_blocks, BLK), jnp.float32),
            jax.ShapeDtypeStruct((user_blocks, BLK), jnp.float32),
        ),
        in_specs=[pl.BlockSpec(memory_space=pltpu.SMEM)] + [vmem] * 5,
        out_specs=(hbm, vmem, vmem),
        scratch_shapes=[
            pltpu.VMEM((blocks, BLK, BLK), jnp.bfloat16),
            dma((blocks // FINAL_GROUP,)),
        ],
        compiler_params=pltpu.CompilerParams(vmem_limit_bytes=14 * 2**20),
    )(in_hbm(ids), scores, user_table, camp_table, camp_duals, user_duals)
    return (
        allocation.reshape(1, 1, blocks, BLK, BLK),
        camp_duals.reshape(-1),
        user_duals.reshape(-1),
    )


def solution(mesh):
    placed = (P("user", "camp"), P("camp", "user"), P("user", "camp", None, None), P("camp"))
    return jax.shard_map(
        functools.partial(on_device, mesh.shape["user"], mesh.shape["camp"]),
        mesh=mesh,
        in_specs=placed,
        out_specs=(P("user", "camp", None, None, None), P("camp"), P("user")),
        check_vma=False,
    )
```
